256 devices in a mesh: rows: 2 (over core), sites: 8 (over z), bond: 16 (over y, x).
Axes of the slice: x: 4, y: 4, z: 8, core: 2. Of those that a mesh axis runs over, the one named last changes fastest.
Arguments:
- boundary_in: float32 [1, 8, 256, 8, 256], P(None, 'sites', None, None, 'bond'), may hold values from -6 to 6
- mpo: float32 [4, 8, 8, 8, 8, 8], P('rows', 'sites'), may hold values from -0.75 to 0.75
- proj: float32 [4, 8, 256, 8, 256], P('rows', 'sites'), may hold values from -0.125 to 0.125
Outputs:
- boundary_out: float32 [2, 1, 8, 256, 8, 256], P('rows', None, 'sites', None, None, 'bond')
The draws below stay inside these ranges and needn't reach their ends.
All inputs are finite; a program needn't handle non-finite values.
Results may differ from the reference program's by a relative error of at most 0.00013.
Values sent between devices are 32-bit elements; how exact they have to be, the bound alone decides.
A program may use at most 64 MiB of HBM per device.

```python
import jax
import jax.numpy as jnp
from jax import lax

CHI = 256
DB = 8
TERMS = 1
GROUP_ROWS = 2
SITES = 8
LROWS = 4
N_ROWS = 2


def levels(own_key, shape, pieces, least, top_value):
    level = 1.0
    for position, parts in pieces:
        steps = jax.random.uniform(jax.random.fold_in(jax.random.fold_in(own_key, 6), position), (parts,), jnp.float32, least / len(pieces), top_value / len(pieces))
        level = level * jnp.repeat(jnp.exp(steps), shape[position] // parts).reshape((-1,) + (1,) * (len(shape) - 1 - position))
    return level


def bell_draw(own_key, dims, spread, bound, split=(), dtype=jnp.bfloat16):
    gain = levels(own_key, dims, split, -0.22, 0.18) if split else 1.0
    result = jax.random.normal(own_key, dims, jnp.float32) * spread * gain
    return jnp.minimum(jnp.maximum(result, -bound), bound).astype(dtype)


def setup_inputs(seed: int = 0) -> dict:
    seeds = jax.random.split(jax.random.key(seed), 4)
    boundary_in = bell_draw(seeds[0], (TERMS, SITES, CHI, DB, CHI), 1.0, 6.0, ((1, 8), (4, 16)), jnp.float32)
    mpo = bell_draw(seeds[1], (LROWS, SITES, DB, DB, DB, DB), (DB * DB) ** -0.5, 0.75, ((0, 2), (1, 8)), jnp.float32)
    proj = bell_draw(seeds[2], (LROWS, SITES, CHI, DB, CHI), (CHI * DB) ** -0.5, 0.125, ((0, 2), (1, 8)), jnp.float32)
    return dict(boundary_in=boundary_in, mpo=mpo, proj=proj)


def absorb_site(packed):
    boundary, left_proj, mpo_row, right_proj = packed
    precise = lax.Precision.HIGHEST
    left_part = jnp.einsum('alx,taub->tlxub', left_proj, boundary, precision=precise)
    mixed_rows = jnp.einsum('tlxub,ludr->txdbr', left_part, mpo_row, precision=precise)
    return jnp.einsum('txdbr,bry->txdy', mixed_rows, right_proj, precision=precise)

def reference(boundary_in, mpo, proj):
    current = jnp.moveaxis(boundary_in, 1, 0)
    results = []
    for group_pos in range(N_ROWS):
        for inner_row in range(GROUP_ROWS):
            lattice_row = GROUP_ROWS * group_pos + inner_row
            right_proj = proj[lattice_row]
            left_proj = jnp.roll(right_proj, 1, axis=0)
            current = lax.map(absorb_site, (current, left_proj, mpo[lattice_row], right_proj))
        square_sum = lax.optimization_barrier(jnp.sum(current * current, axis=(2, 3, 4), keepdims=True))
        current = current / jnp.sqrt(square_sum / (CHI * DB * CHI) + 1e-06)
        results.append(jnp.moveaxis(current, 0, 1))
    return jnp.stack(results)
```

```python
import functools

import jax
import jax.numpy as jnp
from jax import lax
from jax.experimental import pallas as pl
from jax.experimental.pallas import tpu as pltpu
from jax.sharding import PartitionSpec as P

MESH = pl.DeviceIdType.MESH
F32 = jnp.float32
BF16 = jnp.bfloat16


def halves(value):
    high = value.astype(BF16)
    return high, (value - high.astype(F32)).astype(BF16)


def dot(lhs, rhs):
    return jnp.dot(lhs, rhs, preferred_element_type=F32)


def low_lanes(rows):
    return lax.broadcasted_iota(jnp.int32, (rows, 128), 1) < 64


def pair_even(first, second):
    return jnp.where(low_lanes(first.shape[0]), first, pltpu.roll(second, 64, 1))


def pair_odd(first, second):
    return jnp.where(low_lanes(first.shape[0]), pltpu.roll(first, 64, 1), second)


def kernel(
    b_ref, p_ref, m_ref, out_ref,
    first_in, gathered, partial_in, partial, slab, squares, own_square, scale_in,
    left_stage, left_packed, left_in, right_raw, mpo_raw,
    left_high, left_low, right_parts, mpo_parts, lhs_rows, mixed_in, mixed_out,
    first_sem, gather_sem, partial_sem, slab_sem, square_sem, scale_sem,
    left_sem, right_sem, mpo_sem, stage_sem,
    first_send, gather_send, partial_send, slab_send, square_send, scale_send,
    left_send, right_send, mpo_send,
):
    core = lax.axis_index("rows")
    site = lax.axis_index("sites")
    bond = lax.axis_index("bond")
    col = lax.rem(bond, 4)
    row = bond // 4
    next_site = lax.rem(site + 1, 8)
    prev_site = lax.rem(site + 7, 8)

    def in_row(step):
        return row * 4 + lax.rem(col + step, 4)

    def in_col(step):
        return lax.rem(row + step, 4) * 4 + col

    def remote(src, dst, send, recv, device):
        return pltpu.make_async_remote_copy(
            src_ref=src, dst_ref=dst, send_sem=send, recv_sem=recv, device_id=device, device_id_type=MESH
        )

    def left_stage_copy(k):
        block = pl.ds(pl.multiple_of((col // 2) * 128, 128), 128)
        return pltpu.make_async_copy(p_ref.at[k, :, :, block], left_stage.at[k], stage_sem.at[k])

    def own_right(k):
        return p_ref.at[k, pl.ds(row * 64, 64)]

    barrier = pltpu.get_barrier_semaphore()
    peers = [(core, site, lax.rem(bond + k, 16)) for k in range(1, 16)]
    peers += [(1 - core, site, bond), (0, next_site, bond), (1, next_site, bond), (0, prev_site, bond), (1, prev_site, bond)]
    for k in range(2):
        left_stage_copy(k).start()
    for peer in peers:
        pl.semaphore_signal(barrier, inc=1, device_id=peer, device_id_type=MESH)
    pl.semaphore_wait(barrier, len(peers))

    def left_send_copy(k, pair, lattice_row):
        return remote(
            left_packed.at[k, pair], left_in.at[lattice_row, pair], left_send.at[k], left_sem.at[lattice_row, pair],
            (1, next_site, bond),
        )

    def pack_left(k, pair):
        first = left_stage[k, :, 2 * pair, :]
        second = left_stage[k, :, 2 * pair + 1, :]
        half = lax.rem(col, 2)

        @pl.when(half == 0)
        def _():
            left_packed[k, pair] = pair_even(first, second)

        @pl.when(half == 1)
        def _():
            left_packed[k, pair] = pair_odd(first, second)

    def square_copy(step):
        return remote(
            own_square, squares.at[bond], square_send, square_sem, (core, site, lax.rem(bond + step, 16))
        )

    def exchange_squares(value):
        own_square[...] = value
        squares[bond] = value
        for step in range(1, 16):
            square_copy(step).start()

    def inverse_scale():
        pltpu.make_async_copy(squares.at[pl.ds(0, 15)], squares.at[pl.ds(0, 15)], square_sem).wait()
        total = jnp.sum(squares[...])
        mean = jnp.full((8, 128), total, F32) / 524288.0
        return 1.0 / jnp.sqrt(mean + 1e-06)

    def fold(value):
        squared = value * value
        acc = jnp.zeros((8, 128), F32)
        for r0 in range(0, value.shape[0], 8):
            for c0 in range(0, 512, 128):
                acc = acc + squared[r0:r0 + 8, c0:c0 + 128]
        return acc

    def write_out(inverse):
        for r0 in (0, 8):
            for pair in range(2):
                for d_pair in range(4):
                    first = slab[2 * pair, r0:r0 + 8, d_pair * 128:d_pair * 128 + 128]
                    second = slab[2 * pair + 1, r0:r0 + 8, d_pair * 128:d_pair * 128 + 128]
                    lanes = slice(pair * 128, pair * 128 + 128)
                    out_ref[2 * d_pair, r0:r0 + 8, lanes] = pair_even(first, second) * inverse
                    out_ref[2 * d_pair + 1, r0:r0 + 8, lanes] = pair_odd(first, second) * inverse

    def wait_squares_sent():
        pltpu.make_async_copy(squares.at[pl.ds(0, 15)], squares.at[pl.ds(0, 15)], square_send).wait()

    def wait_left_sent():
        for k in range(2):
            pltpu.make_async_copy(left_packed.at[k], left_packed.at[k], left_send.at[k]).wait()

    @pl.when(core == 0)
    def _():
        partner = (1, site, bond)
        right_copies = [remote(own_right(k), right_raw.at[k], right_send.at[k], right_sem.at[k], partner) for k in range(2)]
        mpo_copies = [remote(m_ref.at[k], mpo_raw.at[k], mpo_send.at[k], mpo_sem.at[k], partner) for k in range(2)]
        for k in range(2):
            left_stage_copy(k).wait()
            for pair in range(4):
                pack_left(k, pair)
                left_send_copy(k, pair, k).start()
            right_copies[k].start()
            mpo_copies[k].start()
        pltpu.make_async_copy(slab, slab, slab_sem).wait()
        acc = jnp.zeros((8, 128), F32)
        for k in range(4):
            acc = acc + fold(slab[k])
        exchange_squares(acc)
        inverse = inverse_scale()
        scale_in[...] = inverse
        scale_copy = remote(scale_in, scale_in, scale_send, scale_sem, partner)
        scale_copy.start()
        write_out(inverse)
        scale_copy.wait_send()
        wait_squares_sent()
        wait_left_sent()
        for k in range(2):
            right_copies[k].wait_send()
            mpo_copies[k].wait_send()

    @pl.when(core == 1)
    def _():
        def prepare_left(lattice_row):
            for pair in range(4):
                pltpu.make_async_copy(
                    left_in.at[lattice_row, pair], left_in.at[lattice_row, pair], left_sem.at[lattice_row, pair]
                ).wait()
                high, low = halves(left_in[lattice_row, pair])
                left_high[:, pair * 128:pair * 128 + 128] = high
                left_low[:, pair * 128:pair * 128 + 128] = low

        def prepare_right(lattice_row):
            pltpu.make_async_copy(right_raw.at[lattice_row], right_raw.at[lattice_row], right_sem.at[lattice_row]).wait()
            turned = right_raw[lattice_row].reshape(512, 256).T
            high, low = halves(turned)
            for c in range(4):
                lanes = slice(c * 128, c * 128 + 128)
                right_parts[c, :, 0:128] = high[:, lanes]
                right_parts[c, :, 128:256] = high[:, lanes]
                right_parts[c, :, 256:384] = low[:, lanes]
            pltpu.make_async_copy(mpo_raw.at[lattice_row], mpo_raw.at[lattice_row], mpo_sem.at[lattice_row]).wait()
            turned = jnp.concatenate([mpo_raw[lattice_row, :, d, :].T for d in range(8)], axis=0)
            high, low = halves(turned)
            mpo_parts[...] = jnp.concatenate([high, high, low], axis=1)

        def first_copy(step):
            return remote(b_ref, first_in.at[col], first_send.at[step - 1], first_sem.at[col], (1, site, in_row(step)))

        pltpu.make_async_copy(b_ref, first_in.at[col], first_sem.at[col]).start()
        for step in (2, 1, 3):
            first_copy(step).start()
        for k in range(2):
            pltpu.make_async_copy(own_right(k), right_raw.at[2 + k], right_sem.at[2 + k]).start()
            pltpu.make_async_copy(m_ref.at[k], mpo_raw.at[2 + k], mpo_sem.at[2 + k]).start()
        for k in range(2):
            left_stage_copy(k).wait()
            for pair in range(4):
                pack_left(k, pair)
        prepare_right(0)
        prepare_left(0)

        def gather_copy(lattice_row, c, step):
            return remote(
                gathered.at[lattice_row, c, col], gathered.at[lattice_row, c, col],
                gather_send.at[lattice_row], gather_sem.at[lattice_row, c], (1, site, in_row(step)),
            )

        def absorb_chunk(lattice_row, c):
            @pl.when(lattice_row == 0)
            def _():
                pltpu.make_async_copy(first_in.at[c], first_in.at[c], first_sem.at[c]).wait()
                for u in range(8):
                    for r0 in (0, 8):
                        for pair in range(2):
                            lanes = slice(pair * 128, pair * 128 + 128)
                            lhs_rows[pair, pl.ds(r0 * 8 + u, 8, stride=8), :] = first_in[c, u, r0:r0 + 8, lanes]

            @pl.when(lattice_row > 0)
            def _():
                source = lattice_row - 1
                three = gathered.at[source, c, pl.ds(0, 3)]
                pltpu.make_async_copy(three, three, gather_sem.at[source, c]).wait()
                for r0 in (0, 8):
                    for pair in range(2):
                        for u_pair in range(4):
                            block = slice(u_pair * 128, u_pair * 128 + 128)
                            first = gathered[source, c, 2 * pair, r0:r0 + 8, block]
                            second = gathered[source, c, 2 * pair + 1, r0:r0 + 8, block]
                            start = r0 * 8 + 2 * u_pair
                            lhs_rows[pair, pl.ds(start, 8, stride=8), :] = pair_even(first, second)
                            lhs_rows[pair, pl.ds(start + 1, 8, stride=8), :] = pair_odd(first, second)

            high, low = halves(jnp.concatenate([lhs_rows[0], lhs_rows[1]], axis=1))
            both = dot(jnp.concatenate([high, low], axis=0), left_high[...])
            left_part = both[0:128] + both[128:256] + dot(high, left_low[...])
            for pair in range(4):
                lanes = slice(pair * 128, pair * 128 + 128)
                first = left_part[0:64, lanes]
                second = left_part[64:128, lanes]
                even = pair_even(first, second)
                odd = pair_odd(first, second)
                for k in range(8):
                    mixed_in[pair * 16:pair * 16 + 8, k * 128:k * 128 + 128] = even[k * 8:k * 8 + 8]
                    mixed_in[pair * 16 + 8:pair * 16 + 16, k * 128:k * 128 + 128] = odd[k * 8:k * 8 + 8]
            high, low = halves(mixed_in[...])
            mixed = dot(mpo_parts[...], jnp.concatenate([high, low, high], axis=0))
            for pair in range(4):
                lanes = slice(pair * 128, pair * 128 + 128)
                for k in range(8):
                    block = slice(k * 128, k * 128 + 128)
                    first = mixed[pair * 16:pair * 16 + 8, block]
                    second = mixed[pair * 16 + 8:pair * 16 + 16, block]
                    mixed_out[k * 8:k * 8 + 8, lanes] = pair_even(first, second)
                    mixed_out[64 + k * 8:64 + k * 8 + 8, lanes] = pair_odd(first, second)
            high, low = halves(mixed_out[...])
            added = dot(right_parts[c], jnp.concatenate([high, low, high], axis=0))

            @pl.when(c == 0)
            def _():
                partial[lattice_row] = added

            @pl.when(c > 0)
            def _():
                partial[lattice_row] += added

        def partial_copy(lattice_row, c, step):
            target_row = lax.rem(row + step, 4)
            rows = pl.ds(pl.multiple_of(target_row * 64 + c * 16, 16), 16)
            return remote(
                partial.at[lattice_row, rows], partial_in.at[lattice_row, c, step - 1],
                partial_send.at[lattice_row], partial_sem.at[lattice_row, c], (1, site, in_col(step)),
            )

        def reduced(lattice_row, c):
            every = partial_in.at[lattice_row, c]
            pltpu.make_async_copy(every, every, partial_sem.at[lattice_row, c]).wait()
            rows = pl.ds(pl.multiple_of(row * 64 + c * 16, 16), 16)
            total = partial[lattice_row, rows, :]
            for k in range(3):
                total = total + partial_in[lattice_row, c, k]
            return total

        def slab_out():
            return remote(gathered.at[1, col], slab, slab_send, slab_sem, (0, site, bond))

        def final_copy(c):
            return remote(gathered.at[3, c, col], slab.at[col], slab_send, slab_sem, (1, site, row * 4 + c))

        @pl.loop(0, 4)
        def _(lattice_row):
            @pl.loop(0, 4)
            def _(c):
                absorb_chunk(lattice_row, c)

            @pl.loop(0, 4)
            def _(c):
                for step in (2, 1, 3):
                    partial_copy(lattice_row, c, step).start()

            @pl.when(lattice_row < 2)
            def _():
                for pair in range(4):
                    left_send_copy(lattice_row, pair, lattice_row + 2).start()

            @pl.when(lattice_row == 2)
            def _():
                slab_out().start()

            @pl.when(lattice_row < 3)
            def _():
                prepare_right(lattice_row + 1)

                @pl.loop(0, 4)
                def _(c):
                    gathered[lattice_row, c, col] = reduced(lattice_row, c)
                    for step in (2, 1, 3):
                        gather_copy(lattice_row, c, step).start()

                prepare_left(lattice_row + 1)

        slab_out().wait_send()
        pltpu.make_async_copy(scale_in, scale_in, scale_sem).wait()
        inverse = scale_in[0:1, 0:1]
        acc = jnp.zeros((8, 128), F32)
        for c in range(4):
            total = reduced(3, c) * inverse
            acc = acc + fold(total)

            @pl.when(col == c)
            def _():
                slab[c] = total

            @pl.when(col != c)
            def _():
                gathered[3, c, col] = total
                final_copy(c).start()

        exchange_squares(acc)
        three = slab.at[pl.ds(0, 3)]
        pltpu.make_async_copy(three, three, slab_sem).wait()
        write_out(inverse_scale())

        pltpu.make_async_copy(three, three, slab_send).wait()
        wait_squares_sent()
        wait_left_sent()
        for step in (1, 2, 3):
            first_copy(step).wait_send()
        for k in range(4):
            sent = partial.at[k, pl.ds(0, 192)]
            pltpu.make_async_copy(sent, sent, partial_send.at[k]).wait()
        for k in range(3):
            sent = gathered.at[k, pl.ds(0, 3)]
            pltpu.make_async_copy(sent, sent, gather_send.at[k]).wait()


def body(boundary_in, mpo, proj):
    b = jnp.transpose(boundary_in[0, 0], (1, 2, 0))
    m = mpo.reshape(2, 64, 8, 8)
    p = proj.reshape(2, 256, 8, 256)
    dma = pltpu.SemaphoreType.DMA
    out = pl.pallas_call(
        kernel,
        out_shape=jax.ShapeDtypeStruct((8, 16, 256), F32),
        in_specs=[pl.BlockSpec(memory_space=pltpu.HBM)] * 3,
        out_specs=pl.BlockSpec(memory_space=pltpu.VMEM),
        scratch_shapes=[
            pltpu.VMEM((4, 8, 16, 256), F32),
            pltpu.VMEM((4, 4, 4, 16, 512), F32),
            pltpu.VMEM((4, 4, 3, 16, 512), F32),
            pltpu.VMEM((4, 256, 512), F32),
            pltpu.VMEM((4, 16, 512), F32),
            pltpu.VMEM((16, 8, 128), F32),
            pltpu.VMEM((8, 128), F32),
            pltpu.VMEM((8, 128), F32),
            pltpu.VMEM((2, 256, 8, 128), F32),
            pltpu.VMEM((2, 4, 256, 128), F32),
            pltpu.VMEM((4, 4, 256, 128), F32),
            pltpu.VMEM((4, 64, 8, 256), F32),
            pltpu.VMEM((4, 64, 8, 8), F32),
            pltpu.VMEM((256, 512), BF16),
            pltpu.VMEM((256, 512), BF16),
            pltpu.VMEM((4, 256, 384), BF16),
            pltpu.VMEM((64, 192), BF16),
            pltpu.VMEM((2, 128, 128), F32),
            pltpu.VMEM((64, 1024), F32),
            pltpu.VMEM((128, 512), F32),
            dma((4,)), dma((3, 4)), dma((4, 4)), dma, dma, dma,
            dma((4, 4)), dma((4,)), dma((4,)), dma((2,)),
            dma((3,)), dma((3,)), dma((4,)), dma, dma, dma,
            dma((2,)), dma((2,)), dma((2,)),
        ],
        compiler_params=pltpu.CompilerParams(
            collective_id=0, has_side_effects=True, vmem_limit_bytes=61 * 1024 * 1024
        ),
        name="absorb",
    )(b, p, m)
    return jnp.transpose(out, (2, 0, 1))[None, None, None]


def solution(mesh):
    return jax.shard_map(
        body,
        mesh=mesh,
        in_specs=(
            P(None, "sites", None, None, "bond"),
            P("rows", "sites", None, None, None, None),
            P("rows", "sites", None, None, None),
        ),
        out_specs=P("rows", None, "sites", None, None, "bond"),
        check_vma=False,
    )
```

```python
import functools

import jax
import jax.numpy as jnp
from jax import lax
from jax.experimental import pallas as pl
from jax.experimental.pallas import tpu as pltpu
from jax.sharding import PartitionSpec as P

MESH = pl.DeviceIdType.MESH
F32 = jnp.float32
BF16 = jnp.bfloat16


def halves(value):
    high = value.astype(BF16)
    return high, (value - high.astype(F32)).astype(BF16)


def dot(lhs, rhs):
    return jnp.dot(lhs, rhs, preferred_element_type=F32)


def low_lanes(rows):
    return lax.broadcasted_iota(jnp.int32, (rows, 128), 1) < 64


def pair_even(first, second):
    return jnp.where(low_lanes(first.shape[0]), first, pltpu.roll(second, 64, 1))


def pair_odd(first, second):
    return jnp.where(low_lanes(first.shape[0]), pltpu.roll(first, 64, 1), second)


def kernel(
    b_ref, p_ref, m_ref, out_ref,
    first_raw, first_packed, first_in, first_left, first_out, turned_rows, gathered, partial_in, partial, slab, squares, own_square, scale_in,
    left_stage, left_packed, left_in, right_raw, mpo_raw,
    left_high, left_low, turned_high, turned_low, right_parts, mpo_parts, lhs_rows, mixed_in, mixed_out,
    raw_sem, first_sem, first_left_sem, first_left_send, open_sem,
    gather_sem, partial_sem, slab_sem, square_sem, scale_sem,
    left_sem, right_sem, mpo_sem, stage_sem,
    ready_sem, first_send, gather_send, partial_send, slab_send, square_send, scale_send,
    left_send, right_send, mpo_send,
):
    core = lax.axis_index("rows")
    site = lax.axis_index("sites")
    bond = lax.axis_index("bond")
    col = lax.rem(bond, 4)
    row = bond // 4
    next_site = lax.rem(site + 1, 8)
    prev_site = lax.rem(site + 7, 8)

    def in_row(step):
        return row * 4 + lax.rem(col + step, 4)

    def in_col(step):
        return lax.rem(row + step, 4) * 4 + col

    def remote(src, dst, send, recv, device):
        return pltpu.make_async_remote_copy(
            src_ref=src, dst_ref=dst, send_sem=send, recv_sem=recv, device_id=device, device_id_type=MESH
        )

    def left_stage_copy(k):
        part = jnp.where((core == 0) & (k == 0), row, col)
        block = pl.ds(pl.multiple_of((part // 2) * 128, 128), 128)
        return pltpu.make_async_copy(p_ref.at[k, :, :, block], left_stage.at[k], stage_sem.at[k])

    def own_right(k):
        return p_ref.at[k, pl.ds(row * 64, 64)]

    barrier = pltpu.get_barrier_semaphore()
    for k in range(2):
        left_stage_copy(k).start()

    def greet(device):
        pl.semaphore_signal(barrier, inc=1, device_id=device, device_id_type=MESH)

    @pl.when(core == 0)
    def _():
        greet((1, site, bond))
        pl.semaphore_wait(barrier, 1)

    @pl.when(core == 1)
    def _():
        greet((0, prev_site, bond))
        for step in range(1, 16):
            greet((1, site, lax.rem(bond + step, 16)))

    def left_send_copy(k, pair, lattice_row):
        return remote(
            left_packed.at[k, pair], left_in.at[lattice_row, pair], left_send.at[k], left_sem.at[lattice_row, pair],
            (1, next_site, bond),
        )

    def pack_left(k, pair):
        first = left_stage[k, :, 2 * pair, :]
        second = left_stage[k, :, 2 * pair + 1, :]
        half = lax.rem(jnp.where((core == 0) & (k == 0), row, col), 2)

        @pl.when(half == 0)
        def _():
            left_packed[k, pair] = pair_even(first, second)

        @pl.when(half == 1)
        def _():
            left_packed[k, pair] = pair_odd(first, second)

    def square_copy(step):
        return remote(
            own_square, squares.at[bond], square_send, square_sem, (core, site, lax.rem(bond + step, 16))
        )

    def exchange_squares(value):
        own_square[...] = value
        squares[bond] = value
        for step in range(1, 16):
            square_copy(step).start()

    def inverse_scale():
        pltpu.make_async_copy(squares.at[pl.ds(0, 15)], squares.at[pl.ds(0, 15)], square_sem).wait()
        total = jnp.sum(squares[...])
        mean = jnp.full((8, 128), total, F32) / 524288.0
        return 1.0 / jnp.sqrt(mean + 1e-06)

    def fold(value):
        squared = value * value
        acc = jnp.zeros((8, 128), F32)
        for r0 in range(0, value.shape[0], 8):
            for c0 in range(0, 512, 128):
                acc = acc + squared[r0:r0 + 8, c0:c0 + 128]
        return acc

    def write_out(inverse):
        for r0 in (0, 8):
            for pair in range(2):
                for d_pair in range(4):
                    first = slab[2 * pair, r0:r0 + 8, d_pair * 128:d_pair * 128 + 128]
                    second = slab[2 * pair + 1, r0:r0 + 8, d_pair * 128:d_pair * 128 + 128]
                    lanes = slice(pair * 128, pair * 128 + 128)
                    out_ref[2 * d_pair, r0:r0 + 8, lanes] = pair_even(first, second) * inverse
                    out_ref[2 * d_pair + 1, r0:r0 + 8, lanes] = pair_odd(first, second) * inverse

    def wait_squares_sent():
        pltpu.make_async_copy(squares.at[pl.ds(0, 15)], squares.at[pl.ds(0, 15)], square_send).wait()

    def wait_left_sent():
        for k in range(2):
            pltpu.make_async_copy(left_packed.at[k], left_packed.at[k], left_send.at[k]).wait()

    @pl.when(core == 0)
    def _():
        partner = (1, site, bond)
        own_left = p_ref.at[0, pl.ds(col * 64, 64)]
        for k in range(2):
            remote(
                own_left.at[:, :, pl.ds(k * 128, 128)], first_left.at[k], first_left_send, first_left_sem.at[k],
                (1, next_site, bond),
            ).start()
        first_right = [
            remote(left_packed.at[0, pair], left_in.at[0, pair], left_send.at[0], left_sem.at[0, pair], partner)
            for pair in range(4)
        ]
        right_copy = remote(own_right(1), right_raw.at[1], right_send, right_sem.at[1], partner)
        mpo_copies = [remote(m_ref.at[k], mpo_raw.at[k], mpo_send.at[k], mpo_sem.at[k], partner) for k in range(2)]
        left_stage_copy(0).wait()
        for pair in range(4):
            pack_left(0, pair)
        pl.semaphore_wait(open_sem, 1)
        pl.semaphore_signal(ready_sem, inc=1, device_id=partner, device_id_type=MESH)
        for pair in range(4):
            first_right[pair].start()
        for k in range(2):
            mpo_copies[k].start()
        left_stage_copy(1).wait()
        for pair in range(4):
            pack_left(1, pair)
            left_send_copy(1, pair, 1).start()
        right_copy.start()
        pltpu.make_async_copy(slab, slab, slab_sem).wait()
        acc = jnp.zeros((8, 128), F32)
        for k in range(4):
            acc = acc + fold(slab[k])
        exchange_squares(acc)
        inverse = inverse_scale()
        scale_in[...] = inverse
        scale_copy = remote(scale_in, scale_in, scale_send, scale_sem, partner)
        scale_copy.start()
        write_out(inverse)
        scale_copy.wait_send()
        wait_squares_sent()
        wait_left_sent()
        right_copy.wait_send()
        for k in range(2):
            mpo_copies[k].wait_send()
        pltpu.make_async_copy(first_left, first_left, first_left_send).wait()

    @pl.when(core == 1)
    def _():
        def prepare_left(lattice_row):
            for pair in range(4):
                pltpu.make_async_copy(
                    left_in.at[lattice_row, pair], left_in.at[lattice_row, pair], left_sem.at[lattice_row, pair]
                ).wait()
                high, low = halves(left_in[lattice_row, pair])
                left_high[:, pair * 128:pair * 128 + 128] = high
                left_low[:, pair * 128:pair * 128 + 128] = low

        def prepare_right(lattice_row):
            pltpu.make_async_copy(right_raw.at[lattice_row], right_raw.at[lattice_row], right_sem.at[lattice_row]).wait()
            turned = right_raw[lattice_row].reshape(512, 256).T
            high, low = halves(turned)
            for c in range(4):
                lanes = slice(c * 128, c * 128 + 128)
                right_parts[c, :, 0:128] = high[:, lanes]
                right_parts[c, :, 128:256] = high[:, lanes]
                right_parts[c, :, 256:384] = low[:, lanes]
            pltpu.make_async_copy(mpo_raw.at[lattice_row], mpo_raw.at[lattice_row], mpo_sem.at[lattice_row]).wait()
            turned = jnp.concatenate([mpo_raw[lattice_row, :, d, :].T for d in range(8)], axis=0)
            high, low = halves(turned)
            mpo_parts[...] = jnp.concatenate([high, high, low], axis=1)

        def first_copy(step):
            target = lax.rem(bond + step, 16)
            return remote(
                first_packed.at[lax.rem(target, 4)], first_in.at[bond], first_send, first_sem, (1, site, target)
            )

        raw_copy = pltpu.make_async_copy(b_ref, first_raw, raw_sem)
        raw_copy.start()
        for k in range(2):
            pltpu.make_async_copy(own_right(k), right_raw.at[2 + k], right_sem.at[2 + k]).start()
            pltpu.make_async_copy(m_ref.at[k], mpo_raw.at[2 + k], mpo_sem.at[2 + k]).start()
        raw_copy.wait()
        for block in range(2):
            for u_pair in range(4):
                first = first_raw[2 * u_pair, :, block * 128:block * 128 + 128]
                second = first_raw[2 * u_pair + 1, :, block * 128:block * 128 + 128]
                lanes = slice(u_pair * 128, u_pair * 128 + 128)
                first_packed[2 * block, :, lanes] = pair_even(first, second)
                first_packed[2 * block + 1, :, lanes] = pair_odd(first, second)
        pltpu.make_async_copy(first_packed.at[col], first_in.at[bond], first_sem).start()
        pl.semaphore_wait(barrier, 16)
        pl.semaphore_signal(open_sem, inc=1, device_id=(0, site, bond), device_id_type=MESH)
        for step in (10, 6, 2, 8, 9, 7, 5, 11, 14, 3, 13, 15, 1, 4, 12):
            first_copy(step).start()

        def mix(rows_high, rows_low, c):
            both = dot(jnp.concatenate([rows_high, rows_low], axis=0), left_high[...])
            left_part = both[0:128] + both[128:256] + dot(rows_high, left_low[...])
            for pair in range(4):
                lanes = slice(pair * 128, pair * 128 + 128)
                first = left_part[0:64, lanes]
                second = left_part[64:128, lanes]
                even = pair_even(first, second)
                odd = pair_odd(first, second)
                for k in range(8):
                    block = slice(k * 128, k * 128 + 128)
                    mixed_in[c, pair * 16:pair * 16 + 8, block] = even[k * 8:k * 8 + 8]
                    mixed_in[c, pair * 16 + 8:pair * 16 + 16, block] = odd[k * 8:k * 8 + 8]
            high, low = halves(mixed_in[c])
            mixed = dot(mpo_parts[...], jnp.concatenate([high, low, high], axis=0))
            for pair in range(4):
                lanes = slice(pair * 128, pair * 128 + 128)
                for k in range(8):
                    block = slice(k * 128, k * 128 + 128)
                    first = mixed[pair * 16:pair * 16 + 8, block]
                    second = mixed[pair * 16 + 8:pair * 16 + 16, block]
                    mixed_out[c, k * 8:k * 8 + 8, lanes] = pair_even(first, second)
                    mixed_out[c, 64 + k * 8:64 + k * 8 + 8, lanes] = pair_odd(first, second)

        def close(lattice_row, c):
            high, low = halves(mixed_out[c])
            added = dot(right_parts[c], jnp.concatenate([high, low, high], axis=0))
            if c == 0:
                partial[lattice_row] = added
            else:
                partial[lattice_row] += added

        def gather_copy(lattice_row, c, step):
            return remote(
                gathered.at[lattice_row, c, col], gathered.at[lattice_row, c, col],
                gather_send.at[lattice_row], gather_sem.at[lattice_row, c], (1, site, in_row(step)),
            )

        def first_row():
            for pair in range(4):
                arrived = left_in.at[0, pair]
                pltpu.make_async_copy(arrived, arrived, left_sem.at[0, pair]).wait()
                turned = left_in[0, pair].T
                for k in range(2):
                    for block in range(2):
                        turned_rows[block, pl.ds(2 * pair + k, 64, stride=8), :] = (
                            turned[k * 64:k * 64 + 64, block * 128:block * 128 + 128]
                        )
            high, low = halves(jnp.concatenate([turned_rows[0], turned_rows[1]], axis=1))
            turned_high[...] = high
            turned_low[...] = low
            pltpu.make_async_copy(mpo_raw.at[0], mpo_raw.at[0], mpo_sem.at[0]).wait()
            turned = mpo_raw[0].reshape(8, 8, 8, 8)
            turned = jnp.concatenate([turned[:, u].reshape(64, 8) for u in range(8)], axis=1)
            high, low = halves(turned)
            mpo_parts[...] = jnp.concatenate([high, high, low], axis=1)
            for k in range(2):
                left_stage_copy(k).wait()
                for pair in range(4):
                    pack_left(k, pair)
            pltpu.make_async_copy(first_in, first_in, first_sem).wait()
            high, low = halves(first_in[...].reshape(256, 512))
            left_high[...] = high
            left_low[...] = low
            for c in range(4):
                rows = slice(c * 128, c * 128 + 128)
                mix(turned_high[rows, :], turned_low[rows, :], c)
            for block in range(2):
                pltpu.make_async_copy(first_left.at[block], first_left.at[block], first_left_sem.at[block]).wait()
                right = jnp.concatenate([first_left[block, :, l, :] for l in range(8)], axis=0)
                right_high, right_low = halves(right)
                high, low = halves(mixed_out[...].reshape(512, 512))
                both = dot(jnp.concatenate([high, low], axis=0), right_high)
                first_out[block] = both[0:512] + both[512:1024] + dot(high, right_low)
                for d_pair in range(4):
                    first = first_out[block, pl.ds(2 * d_pair, 64, stride=8), :]
                    second = first_out[block, pl.ds(2 * d_pair + 1, 64, stride=8), :]
                    lanes = slice(d_pair * 128, d_pair * 128 + 128)
                    partial[0, block * 128:block * 128 + 64, lanes] = pair_even(first, second)
                    partial[0, block * 128 + 64:block * 128 + 128, lanes] = pair_odd(first, second)

        def place_rows(lattice_row, c):
            source = lattice_row - 1
            three = gathered.at[source, c, pl.ds(0, 3)]
            pltpu.make_async_copy(three, three, gather_sem.at[source, c]).wait()
            for r0 in (0, 8):
                for pair in range(2):
                    for u_pair in range(4):
                        block = slice(u_pair * 128, u_pair * 128 + 128)
                        first = gathered[source, c, 2 * pair, r0:r0 + 8, block]
                        second = gathered[source, c, 2 * pair + 1, r0:r0 + 8, block]
                        start = r0 * 8 + 2 * u_pair
                        lhs_rows[pair, pl.ds(start, 8, stride=8), :] = pair_even(first, second)
                        lhs_rows[pair, pl.ds(start + 1, 8, stride=8), :] = pair_odd(first, second)
            return halves(jnp.concatenate([lhs_rows[0], lhs_rows[1]], axis=1))

        def later_row(lattice_row):
            for c in range(4):
                high, low = place_rows(lattice_row, c)
                mix(high, low, c)
                if c > 0:
                    close(lattice_row, c - 1)
            close(lattice_row, 3)

        def partial_copy(lattice_row, c, step):
            is_first = lattice_row == 0
            target = lax.rem(jnp.where(is_first, col, row) + step, 4)
            rows = pl.ds(pl.multiple_of(target * 64 + c * 16, 16), 16)
            device = jnp.where(is_first, in_row(step), in_col(step))
            return remote(
                partial.at[lattice_row, rows], partial_in.at[lattice_row, c, step - 1],
                partial_send.at[lattice_row], partial_sem.at[lattice_row, c], (1, site, device),
            )

        def reduced(lattice_row, c):
            every = partial_in.at[lattice_row, c]
            pltpu.make_async_copy(every, every, partial_sem.at[lattice_row, c]).wait()
            own = jnp.where(lattice_row == 0, col, row)
            rows = pl.ds(pl.multiple_of(own * 64 + c * 16, 16), 16)
            total = partial[lattice_row, rows, :]
            for k in range(3):
                total = total + partial_in[lattice_row, c, k]
            return total

        def slab_out():
            return remote(gathered.at[1, col], slab, slab_send, slab_sem, (0, site, bond))

        def final_copy(c):
            return remote(gathered.at[3, c, col], slab.at[col], slab_send, slab_sem, (1, site, row * 4 + c))

        @pl.loop(0, 4)
        def _(lattice_row):
            @pl.when(lattice_row == 0)
            def _():
                first_row()

            @pl.when(lattice_row > 0)
            def _():
                later_row(lattice_row)

            @pl.loop(0, 4)
            def _(c):
                for step in (2, 1, 3):
                    partial_copy(lattice_row, c, step).start()

            @pl.when(lattice_row == 0)
            def _():
                pl.semaphore_wait(ready_sem, 1)

            @pl.when(lattice_row < 2)
            def _():
                for pair in range(4):
                    left_send_copy(lattice_row, pair, lattice_row + 2).start()

            @pl.when(lattice_row == 2)
            def _():
                slab_out().start()

            @pl.when(lattice_row < 3)
            def _():
                prepare_right(lattice_row + 1)

                @pl.loop(0, 4)
                def _(c):
                    gathered[lattice_row, c, col] = reduced(lattice_row, c)
                    for step in (2, 1, 3):
                        gather_copy(lattice_row, c, step).start()

                prepare_left(lattice_row + 1)

        slab_out().wait_send()
        pltpu.make_async_copy(scale_in, scale_in, scale_sem).wait()
        inverse = scale_in[0:1, 0:1]
        acc = jnp.zeros((8, 128), F32)
        for c in range(4):
            total = reduced(3, c) * inverse
            acc = acc + fold(total)

            @pl.when(col == c)
            def _():
                slab[c] = total

            @pl.when(col != c)
            def _():
                gathered[3, c, col] = total
                final_copy(c).start()

        exchange_squares(acc)
        three = slab.at[pl.ds(0, 3)]
        pltpu.make_async_copy(three, three, slab_sem).wait()
        write_out(inverse_scale())

        pltpu.make_async_copy(three, three, slab_send).wait()
        wait_squares_sent()
        wait_left_sent()
        pltpu.make_async_copy(first_in.at[pl.ds(0, 15)], first_in.at[pl.ds(0, 15)], first_send).wait()
        for k in range(4):
            sent = partial.at[k, pl.ds(0, 192)]
            pltpu.make_async_copy(sent, sent, partial_send.at[k]).wait()
        for k in range(3):
            sent = gathered.at[k, pl.ds(0, 3)]
            pltpu.make_async_copy(sent, sent, gather_send.at[k]).wait()


def body(boundary_in, mpo, proj):
    b = jnp.transpose(boundary_in[0, 0], (1, 2, 0))
    m = mpo.reshape(2, 64, 8, 8)
    p = proj.reshape(2, 256, 8, 256)
    b, m, p = (pltpu.with_memory_space_constraint(v, pltpu.HBM) for v in (b, m, p))
    dma = pltpu.SemaphoreType.DMA
    out = pl.pallas_call(
        kernel,
        out_shape=jax.ShapeDtypeStruct((8, 16, 256), F32),
        in_specs=[pl.BlockSpec(memory_space=pltpu.HBM)] * 3,
        out_specs=pl.BlockSpec(memory_space=pltpu.VMEM),
        scratch_shapes=[
            pltpu.VMEM((8, 16, 256), F32),
            pltpu.VMEM((4, 16, 512), F32),
            pltpu.VMEM((16, 16, 512), F32),
            pltpu.VMEM((2, 64, 8, 128), F32),
            pltpu.VMEM((2, 512, 128), F32),
            pltpu.VMEM((2, 512, 128), F32),
            pltpu.VMEM((4, 4, 4, 16, 512), F32),
            pltpu.VMEM((4, 4, 3, 16, 512), F32),
            pltpu.VMEM((4, 256, 512), F32),
            pltpu.VMEM((4, 16, 512), F32),
            pltpu.VMEM((16, 8, 128), F32),
            pltpu.VMEM((8, 128), F32),
            pltpu.VMEM((8, 128), F32),
            pltpu.VMEM((2, 256, 8, 128), F32),
            pltpu.VMEM((2, 4, 256, 128), F32),
            pltpu.VMEM((4, 4, 256, 128), F32),
            pltpu.VMEM((4, 64, 8, 256), F32),
            pltpu.VMEM((4, 64, 8, 8), F32),
            pltpu.VMEM((256, 512), BF16),
            pltpu.VMEM((256, 512), BF16),
            pltpu.VMEM((512, 256), BF16),
            pltpu.VMEM((512, 256), BF16),
            pltpu.VMEM((4, 256, 384), BF16),
            pltpu.VMEM((64, 192), BF16),
            pltpu.VMEM((2, 128, 128), F32),
            pltpu.VMEM((4, 64, 1024), F32),
            pltpu.VMEM((4, 128, 512), F32),
            dma, dma, dma((2,)), dma, pltpu.SemaphoreType.REGULAR,
            dma((3, 4)), dma((4, 4)), dma, dma, dma,
            dma((4, 4)), dma((4,)), dma((4,)), dma((2,)),
            pltpu.SemaphoreType.REGULAR,
            dma, dma((3,)), dma((4,)), dma, dma, dma,
            dma((2,)), dma, dma((2,)),
        ],
        compiler_params=pltpu.CompilerParams(
            collective_id=0, has_side_effects=True, vmem_limit_bytes=40 * 1024 * 1024
        ),
        name="absorb",
    )(b, p, m)
    return jnp.transpose(out, (2, 0, 1))[None, None, None]


def solution(mesh):
    return jax.shard_map(
        body,
        mesh=mesh,
        in_specs=(
            P(None, "sites", None, None, "bond"),
            P("rows", "sites", None, None, None, None),
            P("rows", "sites", None, None, None),
        ),
        out_specs=P("rows", None, "sites", None, None, "bond"),
        check_vma=False,
    )
```

```python
import functools

import jax
import jax.numpy as jnp
from jax import lax
from jax.experimental import pallas as pl
from jax.experimental.pallas import tpu as pltpu
from jax.sharding import PartitionSpec as P

MESH = pl.DeviceIdType.MESH
F32 = jnp.float32
BF16 = jnp.bfloat16


def halves(value):
    high = value.astype(BF16)
    return high, (value - high.astype(F32)).astype(BF16)


def dot(lhs, rhs):
    return jnp.dot(lhs, rhs, preferred_element_type=F32)


def low_lanes(rows):
    return lax.broadcasted_iota(jnp.int32, (rows, 128), 1) < 64


def pair_even(first, second):
    return jnp.where(low_lanes(first.shape[0]), first, pltpu.roll(second, 64, 1))


def pair_odd(first, second):
    return jnp.where(low_lanes(first.shape[0]), pltpu.roll(first, 64, 1), second)


def kernel(
    b_ref, p_ref, m_ref, out_ref,
    first_raw, first_packed, first_in, first_left, first_out, turned_rows, gathered, partial_in, partial, slab, squares, own_square, scale_in,
    left_stage, left_packed, left_in, right_raw, mpo_raw,
    left_high, left_low, turned_high, turned_low, right_parts, mpo_parts, lhs_rows, mixed_in, mixed_out,
    raw_sem, first_sem, first_left_sem, first_left_send, lead_sem, lead_send, tail_sem, open_sem,
    gather_sem, partial_sem, slab_sem, square_sem, scale_sem,
    left_sem, right_sem, mpo_sem, stage_sem,
    ready_sem, first_send, gather_send, partial_send, slab_send, square_send, scale_send,
    left_send, right_send, mpo_send,
):
    core = lax.axis_index("rows")
    site = lax.axis_index("sites")
    bond = lax.axis_index("bond")
    col = lax.rem(bond, 4)
    row = bond // 4
    next_site = lax.rem(site + 1, 8)
    prev_site = lax.rem(site + 7, 8)

    def in_row(step):
        return row * 4 + lax.rem(col + step, 4)

    def in_col(step):
        return lax.rem(row + step, 4) * 4 + col

    def remote(src, dst, send, recv, device):
        return pltpu.make_async_remote_copy(
            src_ref=src, dst_ref=dst, send_sem=send, recv_sem=recv, device_id=device, device_id_type=MESH
        )

    def left_stage_copy(k):
        part = jnp.where((core == 0) & (k == 0), row, col)
        block = pl.ds(pl.multiple_of((part // 2) * 128, 128), 128)
        return pltpu.make_async_copy(p_ref.at[k, :, :, block], left_stage.at[k], stage_sem.at[k])

    def own_right(k):
        return p_ref.at[k, pl.ds(row * 64, 64)]

    barrier = pltpu.get_barrier_semaphore()
    for k in range(2):
        left_stage_copy(k).start()

    def greet(device):
        pl.semaphore_signal(barrier, inc=1, device_id=device, device_id_type=MESH)

    @pl.when(core == 0)
    def _():
        greet((1, site, bond))
        pl.semaphore_wait(barrier, 1)

    @pl.when(core == 1)
    def _():
        greet((0, prev_site, bond))
        for step in range(1, 16):
            greet((1, site, lax.rem(bond + step, 16)))

    def left_send_copy(k, pair, lattice_row):
        return remote(
            left_packed.at[k, pair], left_in.at[lattice_row, pair], left_send.at[k], left_sem.at[lattice_row, pair],
            (1, next_site, bond),
        )

    def pack_left(k, pair):
        first = left_stage[k, :, 2 * pair, :]
        second = left_stage[k, :, 2 * pair + 1, :]
        half = lax.rem(jnp.where((core == 0) & (k == 0), row, col), 2)

        @pl.when(half == 0)
        def _():
            left_packed[k, pair] = pair_even(first, second)

        @pl.when(half == 1)
        def _():
            left_packed[k, pair] = pair_odd(first, second)

    far_first = [(2, 2), (2, 1), (2, 3), (1, 2), (3, 2), (1, 1), (1, 3), (3, 1), (3, 3), (2, 0), (0, 2), (1, 0), (3, 0), (0, 1), (0, 3)]

    def other(offset):
        return lax.rem(row + offset[0], 4) * 4 + lax.rem(col + offset[1], 4)

    def square_copy(offset):
        return remote(own_square, squares.at[bond], square_send, square_sem, (core, site, other(offset)))

    def exchange_squares(value):
        own_square[...] = value
        squares[bond] = value
        for offset in far_first:
            square_copy(offset).start()

    def inverse_scale():
        pltpu.make_async_copy(squares.at[pl.ds(0, 15)], squares.at[pl.ds(0, 15)], square_sem).wait()
        total = jnp.sum(squares[...])
        mean = jnp.full((8, 128), total, F32) / 524288.0
        return 1.0 / jnp.sqrt(mean + 1e-06)

    def fold(value):
        squared = value * value
        acc = jnp.zeros((8, 128), F32)
        for r0 in range(0, value.shape[0], 8):
            for c0 in range(0, 512, 128):
                acc = acc + squared[r0:r0 + 8, c0:c0 + 128]
        return acc

    def write_out(inverse):
        pieces = []
        for r0 in (0, 8):
            for pair in range(2):
                for d_pair in range(4):
                    first = slab[2 * pair, r0:r0 + 8, d_pair * 128:d_pair * 128 + 128]
                    second = slab[2 * pair + 1, r0:r0 + 8, d_pair * 128:d_pair * 128 + 128]
                    lanes = slice(pair * 128, pair * 128 + 128)
                    pieces.append((2 * d_pair, r0, lanes, pair_even(first, second)))
                    pieces.append((2 * d_pair + 1, r0, lanes, pair_odd(first, second)))
        scale = inverse()
        for d, r0, lanes, value in pieces:
            out_ref[d, r0:r0 + 8, lanes] = value * scale

    def wait_squares_sent():
        pltpu.make_async_copy(squares.at[pl.ds(0, 15)], squares.at[pl.ds(0, 15)], square_send).wait()

    def wait_left_sent():
        for k in range(2):
            pltpu.make_async_copy(left_packed.at[k], left_packed.at[k], left_send.at[k]).wait()

    @pl.when(core == 0)
    def _():
        partner = (1, site, bond)
        for k in range(3):
            quarter = lax.rem(row + k, 4)
            lanes = pl.ds(pl.multiple_of((quarter // 2) * 128, 128), 128)
            size = 16 if k == 0 else 32
            for start in range(0, 32, size):
                rows = pl.ds(col * 64 + lax.rem(quarter, 2) * 32 + start, size)
                remote(
                    p_ref.at[0, rows, :, lanes], first_left.at[quarter, pl.ds(start, size)], first_left_send,
                    lead_sem.at[start // 16] if k == 0 else first_left_sem, (1, next_site, bond),
                ).start()
        first_right = [
            remote(left_packed.at[0, pair], left_in.at[0, pair], left_send.at[0], left_sem.at[0, pair], partner)
            for pair in range(4)
        ]
        right_copy = remote(own_right(1), right_raw.at[1], right_send, right_sem.at[1], partner)
        mpo_copies = [remote(m_ref.at[k], mpo_raw.at[k], mpo_send.at[k], mpo_sem.at[k], partner) for k in range(2)]
        left_stage_copy(0).wait()
        for pair in range(4):
            pack_left(0, pair)
        pl.semaphore_wait(open_sem, 1)
        pl.semaphore_signal(ready_sem, inc=1, device_id=partner, device_id_type=MESH)
        for pair in range(4):
            first_right[pair].start()
        for k in range(2):
            mpo_copies[k].start()
        left_stage_copy(1).wait()
        for pair in range(4):
            pack_left(1, pair)
            left_send_copy(1, pair, 1).start()
        right_copy.start()
        pltpu.make_async_copy(slab, slab, slab_sem).wait()
        acc = jnp.zeros((8, 128), F32)
        for k in range(4):
            acc = acc + fold(slab[k])
        exchange_squares(acc)
        inverse = inverse_scale()
        scale_in[...] = inverse
        scale_copy = remote(scale_in, scale_in, scale_send, scale_sem, partner)
        scale_copy.start()
        write_out(lambda: inverse)
        scale_copy.wait_send()
        wait_squares_sent()
        wait_left_sent()
        right_copy.wait_send()
        for k in range(2):
            mpo_copies[k].wait_send()
        sent = first_left.at[pl.ds(0, 3)]
        pltpu.make_async_copy(sent, sent, first_left_send).wait()

    @pl.when(core == 1)
    def _():
        def prepare_left(lattice_row):
            for pair in range(4):
                pltpu.make_async_copy(
                    left_in.at[lattice_row, pair], left_in.at[lattice_row, pair], left_sem.at[lattice_row, pair]
                ).wait()
                high, low = halves(left_in[lattice_row, pair])
                left_high[:, pair * 128:pair * 128 + 128] = high
                left_low[:, pair * 128:pair * 128 + 128] = low

        def prepare_right(lattice_row):
            pltpu.make_async_copy(right_raw.at[lattice_row], right_raw.at[lattice_row], right_sem.at[lattice_row]).wait()
            turned = right_raw[lattice_row].reshape(512, 256).T
            starts = [target * 64 + piece * 8 for piece in range(8) for target in range(4)]
            turned = jnp.concatenate([turned[start:start + 8] for start in starts], axis=0)
            high, low = halves(turned)
            for c in range(4):
                lanes = slice(c * 128, c * 128 + 128)
                right_parts[c, :, 0:128] = high[:, lanes]
                right_parts[c, :, 128:256] = high[:, lanes]
                right_parts[c, :, 256:384] = low[:, lanes]
            pltpu.make_async_copy(mpo_raw.at[lattice_row], mpo_raw.at[lattice_row], mpo_sem.at[lattice_row]).wait()
            turned = jnp.concatenate([mpo_raw[lattice_row, :, d, :].T for d in range(8)], axis=0)
            high, low = halves(turned)
            mpo_parts[...] = jnp.concatenate([high, high, low], axis=1)

        def first_copy(offset):
            target = other(offset)
            return remote(
                first_packed.at[lax.rem(target, 4)], first_in.at[bond], first_send, first_sem, (1, site, target)
            )

        raw_copy = pltpu.make_async_copy(b_ref, first_raw, raw_sem)
        raw_copy.start()
        for k in range(2):
            pltpu.make_async_copy(own_right(k), right_raw.at[2 + k], right_sem.at[2 + k]).start()
            pltpu.make_async_copy(m_ref.at[k], mpo_raw.at[2 + k], mpo_sem.at[2 + k]).start()
        raw_copy.wait()
        for block in range(2):
            for u_pair in range(4):
                first = first_raw[2 * u_pair, :, block * 128:block * 128 + 128]
                second = first_raw[2 * u_pair + 1, :, block * 128:block * 128 + 128]
                lanes = slice(u_pair * 128, u_pair * 128 + 128)
                first_packed[2 * block, :, lanes] = pair_even(first, second)
                first_packed[2 * block + 1, :, lanes] = pair_odd(first, second)
        pltpu.make_async_copy(first_packed.at[col], first_in.at[bond], first_sem).start()
        pl.semaphore_wait(barrier, 16)
        pl.semaphore_signal(open_sem, inc=1, device_id=(0, site, bond), device_id_type=MESH)
        for offset in far_first:
            first_copy(offset).start()

        def mix(rows_high, rows_low, c):
            both = dot(jnp.concatenate([rows_high, rows_low], axis=0), left_high[...])
            left_part = both[0:128] + both[128:256] + dot(rows_high, left_low[...])
            for pair in range(4):
                lanes = slice(pair * 128, pair * 128 + 128)
                first = left_part[0:64, lanes]
                second = left_part[64:128, lanes]
                even = pair_even(first, second)
                odd = pair_odd(first, second)
                for k in range(8):
                    block = slice(k * 128, k * 128 + 128)
                    mixed_in[c, pair * 16:pair * 16 + 8, block] = even[k * 8:k * 8 + 8]
                    mixed_in[c, pair * 16 + 8:pair * 16 + 16, block] = odd[k * 8:k * 8 + 8]
            high, low = halves(mixed_in[c])
            mixed = dot(mpo_parts[...], jnp.concatenate([high, low, high], axis=0))
            for pair in range(4):
                lanes = slice(pair * 128, pair * 128 + 128)
                for k in range(8):
                    block = slice(k * 128, k * 128 + 128)
                    first = mixed[pair * 16:pair * 16 + 8, block]
                    second = mixed[pair * 16 + 8:pair * 16 + 16, block]
                    mixed_out[c, k * 8:k * 8 + 8, lanes] = pair_even(first, second)
                    mixed_out[c, 64 + k * 8:64 + k * 8 + 8, lanes] = pair_odd(first, second)

        def close(lattice_row, c, start=0, size=256):
            high, low = halves(mixed_out[c])
            rows = slice(start, start + size)
            added = dot(right_parts[c, rows, :], jnp.concatenate([high, low, high], axis=0))
            if c == 0:
                partial[lattice_row, rows, :] = added
            else:
                partial[lattice_row, rows, :] += added

        def gather_copy(lattice_row, c, step):
            piece = gathered.at[lattice_row, c // 2, col, pl.ds(pl.multiple_of(lax.rem(c, 2) * 8, 8), 8)]
            return remote(
                piece, piece, gather_send.at[lattice_row], gather_sem.at[lattice_row, c // 2], (1, site, in_row(step))
            )

        def pass_on(k):
            lead = first_left.at[row, pl.ds(k * 16, 16)]
            return remote(lead, lead, lead_send, tail_sem, (1, site, in_col(1)))

        def first_row():
            for pair in range(4):
                arrived = left_in.at[0, pair]
                pltpu.make_async_copy(arrived, arrived, left_sem.at[0, pair]).wait()
                turned = left_in[0, pair].T
                for k in range(2):
                    for block in range(2):
                        turned_rows[block, pl.ds(2 * pair + k, 64, stride=8), :] = (
                            turned[k * 64:k * 64 + 64, block * 128:block * 128 + 128]
                        )
            high, low = halves(jnp.concatenate([turned_rows[0], turned_rows[1]], axis=1))
            turned_high[...] = high
            turned_low[...] = low
            pltpu.make_async_copy(mpo_raw.at[0], mpo_raw.at[0], mpo_sem.at[0]).wait()
            turned = mpo_raw[0].reshape(8, 8, 8, 8)
            turned = jnp.concatenate([turned[:, u].reshape(64, 8) for u in range(8)], axis=1)
            high, low = halves(turned)
            mpo_parts[...] = jnp.concatenate([high, high, low], axis=1)
            for k in range(2):
                left_stage_copy(k).wait()
                for pair in range(4):
                    pack_left(k, pair)
            for k in range(2):
                lead = first_left.at[row, pl.ds(k * 16, 16)]
                pltpu.make_async_copy(lead, lead, lead_sem.at[k]).wait()
                pass_on(k).start()
            pltpu.make_async_copy(first_in, first_in, first_sem).wait()
            high, low = halves(first_in[...].reshape(256, 512))
            left_high[...] = high
            left_low[...] = low
            for c in range(4):
                rows = slice(c * 128, c * 128 + 128)
                mix(turned_high[rows, :], turned_low[rows, :], c)
            pltpu.make_async_copy(first_left.at[pl.ds(0, 2)], first_left.at[pl.ds(0, 2)], first_left_sem).wait()
            pltpu.make_async_copy(first_left.at[0], first_left.at[0], tail_sem).wait()
            for block in range(2):
                right = jnp.concatenate(
                    [first_left[2 * block + k, :, l, :] for l in range(8) for k in range(2)], axis=0
                )
                right_high, right_low = halves(right)
                high, low = halves(mixed_out[...].reshape(512, 512))
                both = dot(jnp.concatenate([high, low], axis=0), right_high)
                first_out[block] = both[0:512] + both[512:1024] + dot(high, right_low)
                for d_pair in range(4):
                    first = first_out[block, pl.ds(2 * d_pair, 64, stride=8), :]
                    second = first_out[block, pl.ds(2 * d_pair + 1, 64, stride=8), :]
                    lanes = slice(d_pair * 128, d_pair * 128 + 128)
                    even = pair_even(first, second)
                    odd = pair_odd(first, second)
                    for piece in range(8):
                        start = piece * 32 + block * 16
                        partial[0, start:start + 8, lanes] = even[piece * 8:piece * 8 + 8]
                        partial[0, start + 8:start + 16, lanes] = odd[piece * 8:piece * 8 + 8]

        def place_rows(lattice_row, c):
            source = lattice_row - 1
            three = gathered.at[source, c, pl.ds(0, 3)]
            pltpu.make_async_copy(three, three, gather_sem.at[source, c]).wait()
            for r0 in (0, 8):
                for pair in range(2):
                    for u_pair in range(4):
                        block = slice(u_pair * 128, u_pair * 128 + 128)
                        first = gathered[source, c, 2 * pair, r0:r0 + 8, block]
                        second = gathered[source, c, 2 * pair + 1, r0:r0 + 8, block]
                        start = r0 * 8 + 2 * u_pair
                        lhs_rows[pair, pl.ds(start, 8, stride=8), :] = pair_even(first, second)
                        lhs_rows[pair, pl.ds(start + 1, 8, stride=8), :] = pair_odd(first, second)
            return halves(jnp.concatenate([lhs_rows[0], lhs_rows[1]], axis=1))

        def later_row(lattice_row):
            for c in range(4):
                high, low = place_rows(lattice_row, c)
                mix(high, low, c)
                if c > 0:
                    close(lattice_row, c - 1)
            close(lattice_row, 3, 0, 64)
            send_partial(lattice_row, 0, 2)
            close(lattice_row, 3, 64, 192)
            send_partial(lattice_row, 2, 8)

        def partial_copy(lattice_row, c, step):
            is_first = lattice_row == 0
            target = lax.rem(jnp.where(is_first, col, row) + step, 4)
            rows = pl.ds(pl.multiple_of(c * 32 + target * 8, 8), 8)
            device = jnp.where(is_first, in_row(step), in_col(step))
            return remote(
                partial.at[lattice_row, rows], partial_in.at[lattice_row, c, step - 1],
                partial_send.at[lattice_row], partial_sem.at[lattice_row, c], (1, site, device),
            )

        def send_partial(lattice_row, begin, end):
            @pl.loop(begin, end)
            def _(c):
                for step in (2, 1, 3):
                    partial_copy(lattice_row, c, step).start()

        def reduced(lattice_row, c):
            every = partial_in.at[lattice_row, c]
            pltpu.make_async_copy(every, every, partial_sem.at[lattice_row, c]).wait()
            own = jnp.where(lattice_row == 0, col, row)
            rows = pl.ds(pl.multiple_of(c * 32 + own * 8, 8), 8)
            total = partial[lattice_row, rows, :]
            for k in range(3):
                total = total + partial_in[lattice_row, c, k]
            return total

        def slab_out():
            return remote(gathered.at[1, col], slab, slab_send, slab_sem, (0, site, bond))

        def final_copy(c):
            return remote(gathered.at[3, c, col], slab.at[col], slab_send, slab_sem, (1, site, row * 4 + c))

        @pl.loop(0, 4)
        def _(lattice_row):
            @pl.when(lattice_row == 0)
            def _():
                first_row()
                send_partial(0, 0, 8)

            @pl.when(lattice_row > 0)
            def _():
                later_row(lattice_row)

            @pl.when(lattice_row == 0)
            def _():
                pl.semaphore_wait(ready_sem, 1)

            @pl.when(lattice_row < 2)
            def _():
                for pair in range(4):
                    left_send_copy(lattice_row, pair, lattice_row + 2).start()

            @pl.when(lattice_row == 2)
            def _():
                slab_out().start()

            @pl.when(lattice_row < 3)
            def _():
                prepare_right(lattice_row + 1)

                @pl.loop(0, 8)
                def _(c):
                    rows = pl.ds(pl.multiple_of(lax.rem(c, 2) * 8, 8), 8)
                    gathered[lattice_row, c // 2, col, rows, :] = reduced(lattice_row, c)
                    for step in (2, 1, 3):
                        gather_copy(lattice_row, c, step).start()

                prepare_left(lattice_row + 1)

        slab_out().wait_send()
        pltpu.make_async_copy(first_left.at[0], first_left.at[0], lead_send).wait()
        pltpu.make_async_copy(scale_in, scale_in, scale_sem).wait()
        inverse = scale_in[0:1, 0:1]
        acc = jnp.zeros((8, 128), F32)
        for c in range(4):
            total = jnp.concatenate([reduced(3, 2 * c), reduced(3, 2 * c + 1)], axis=0) * inverse
            acc = acc + fold(total)

            @pl.when(col == c)
            def _():
                slab[c] = total

            @pl.when(col != c)
            def _():
                gathered[3, c, col] = total
                if c < 3:
                    final_copy(c).start()

        exchange_squares(acc)

        @pl.when(col != 3)
        def _():
            final_copy(3).start()

        three = slab.at[pl.ds(0, 3)]
        pltpu.make_async_copy(three, three, slab_sem).wait()
        write_out(inverse_scale)

        pltpu.make_async_copy(three, three, slab_send).wait()
        wait_squares_sent()
        wait_left_sent()
        pltpu.make_async_copy(first_in.at[pl.ds(0, 15)], first_in.at[pl.ds(0, 15)], first_send).wait()
        for k in range(4):
            sent = partial.at[k, pl.ds(0, 192)]
            pltpu.make_async_copy(sent, sent, partial_send.at[k]).wait()
        for k in range(3):
            sent = gathered.at[k, pl.ds(0, 3)]
            pltpu.make_async_copy(sent, sent, gather_send.at[k]).wait()


def body(boundary_in, mpo, proj):
    b = jnp.transpose(boundary_in[0, 0], (1, 2, 0))
    m = mpo.reshape(2, 64, 8, 8)
    p = proj.reshape(2, 256, 8, 256)
    b, m, p = (pltpu.with_memory_space_constraint(v, pltpu.HBM) for v in (b, m, p))
    dma = pltpu.SemaphoreType.DMA
    out = pl.pallas_call(
        kernel,
        out_shape=jax.ShapeDtypeStruct((8, 16, 256), F32),
        in_specs=[pl.BlockSpec(memory_space=pltpu.HBM)] * 3,
        out_specs=pl.BlockSpec(memory_space=pltpu.VMEM),
        scratch_shapes=[
            pltpu.VMEM((8, 16, 256), F32),
            pltpu.VMEM((4, 16, 512), F32),
            pltpu.VMEM((16, 16, 512), F32),
            pltpu.VMEM((4, 32, 8, 128), F32),
            pltpu.VMEM((2, 512, 128), F32),
            pltpu.VMEM((2, 512, 128), F32),
            pltpu.VMEM((4, 4, 4, 16, 512), F32),
            pltpu.VMEM((4, 8, 3, 8, 512), F32),
            pltpu.VMEM((4, 256, 512), F32),
            pltpu.VMEM((4, 16, 512), F32),
            pltpu.VMEM((16, 8, 128), F32),
            pltpu.VMEM((8, 128), F32),
            pltpu.VMEM((8, 128), F32),
            pltpu.VMEM((2, 256, 8, 128), F32),
            pltpu.VMEM((2, 4, 256, 128), F32),
            pltpu.VMEM((4, 4, 256, 128), F32),
            pltpu.VMEM((4, 64, 8, 256), F32),
            pltpu.VMEM((4, 64, 8, 8), F32),
            pltpu.VMEM((256, 512), BF16),
            pltpu.VMEM((256, 512), BF16),
            pltpu.VMEM((512, 256), BF16),
            pltpu.VMEM((512, 256), BF16),
            pltpu.VMEM((4, 256, 384), BF16),
            pltpu.VMEM((64, 192), BF16),
            pltpu.VMEM((2, 128, 128), F32),
            pltpu.VMEM((4, 64, 1024), F32),
            pltpu.VMEM((4, 128, 512), F32),
            dma, dma, dma, dma, dma((2,)), dma, dma, pltpu.SemaphoreType.REGULAR,
            dma((3, 4)), dma((4, 8)), dma, dma, dma,
            dma((4, 4)), dma((4,)), dma((4,)), dma((2,)),
            pltpu.SemaphoreType.REGULAR,
            dma, dma((3,)), dma((4,)), dma, dma, dma,
            dma((2,)), dma, dma((2,)),
        ],
        compiler_params=pltpu.CompilerParams(
            collective_id=0, has_side_effects=True, vmem_limit_bytes=40 * 1024 * 1024
        ),
        name="absorb",
    )(b, p, m)
    return jnp.transpose(out, (2, 0, 1))[None, None, None]


def solution(mesh):
    return jax.shard_map(
        body,
        mesh=mesh,
        in_specs=(
            P(None, "sites", None, None, "bond"),
            P("rows", "sites", None, None, None, None),
            P("rows", "sites", None, None, None),
        ),
        out_specs=P("rows", None, "sites", None, None, "bond"),
        check_vma=False,
    )
```

```python
import functools

import jax
import jax.numpy as jnp
from jax import lax
from jax.experimental import pallas as pl
from jax.experimental.pallas import tpu as pltpu
from jax.sharding import PartitionSpec as P

MESH = pl.DeviceIdType.MESH
F32 = jnp.float32
BF16 = jnp.bfloat16


def halves(value):
    high = value.astype(BF16)
    return high, (value - high.astype(F32)).astype(BF16)


def dot(lhs, rhs):
    return jnp.dot(lhs, rhs, preferred_element_type=F32)


def low_lanes(rows):
    return lax.broadcasted_iota(jnp.int32, (rows, 128), 1) < 64


def pair_even(first, second):
    return jnp.where(low_lanes(first.shape[0]), first, pltpu.roll(second, 64, 1))


def pair_odd(first, second):
    return jnp.where(low_lanes(first.shape[0]), pltpu.roll(first, 64, 1), second)


def kernel(
    b_ref, p_ref, m_ref, out_ref,
    first_raw, first_packed, first_in, first_left, first_out, turned_rows, gathered, partial_in, partial, slab, squares, own_square, scale_in,
    left_stage, left_packed, left_in, right_raw, mpo_raw,
    left_high, left_low, turned_high, turned_low, right_parts, mpo_parts, lhs_rows, mixed_in, mixed_out,
    raw_sem, first_sem, first_left_sem, first_left_send, lead_sem, lead_send, tail_sem, open_sem,
    gather_sem, partial_sem, slab_sem, square_sem, scale_sem,
    left_sem, right_sem, mpo_sem, stage_sem,
    ready_sem, first_send, gather_send, partial_send, slab_send, square_send, scale_send,
    left_send, right_send, mpo_send,
):
    core = lax.axis_index("rows")
    site = lax.axis_index("sites")
    bond = lax.axis_index("bond")
    col = lax.rem(bond, 4)
    row = bond // 4
    next_site = lax.rem(site + 1, 8)
    prev_site = lax.rem(site + 7, 8)

    def in_row(step):
        return row * 4 + lax.rem(col + step, 4)

    def in_col(step):
        return lax.rem(row + step, 4) * 4 + col

    def remote(src, dst, send, recv, device):
        return pltpu.make_async_remote_copy(
            src_ref=src, dst_ref=dst, send_sem=send, recv_sem=recv, device_id=device, device_id_type=MESH
        )

    def left_stage_copy(k):
        part = jnp.where((core == 0) & (k == 0), row, col)
        block = pl.ds(pl.multiple_of((part // 2) * 128, 128), 128)
        return pltpu.make_async_copy(p_ref.at[k, :, :, block], left_stage.at[k], stage_sem.at[k])

    def own_right(k):
        return p_ref.at[k, pl.ds(row * 64, 64)]

    barrier = pltpu.get_barrier_semaphore()
    for k in range(2):
        left_stage_copy(k).start()

    def greet(device):
        pl.semaphore_signal(barrier, inc=1, device_id=device, device_id_type=MESH)

    @pl.when(core == 0)
    def _():
        greet((1, site, bond))
        pl.semaphore_wait(barrier, 1)

    @pl.when(core == 1)
    def _():
        greet((0, prev_site, bond))
        for step in range(1, 16):
            greet((1, site, lax.rem(bond + step, 16)))

    def left_send_copy(k, pair, lattice_row):
        return remote(
            left_packed.at[k, pair], left_in.at[lattice_row, pair], left_send.at[k], left_sem.at[lattice_row, pair],
            (1, next_site, bond),
        )

    def pack_left(k, pair):
        first = left_stage[k, :, 2 * pair, :]
        second = left_stage[k, :, 2 * pair + 1, :]
        half = lax.rem(jnp.where((core == 0) & (k == 0), row, col), 2)

        @pl.when(half == 0)
        def _():
            left_packed[k, pair] = pair_even(first, second)

        @pl.when(half == 1)
        def _():
            left_packed[k, pair] = pair_odd(first, second)

    far_first = [(2, 2), (2, 1), (2, 3), (1, 2), (3, 2), (1, 1), (1, 3), (3, 1), (3, 3), (2, 0), (0, 2), (1, 0), (3, 0), (0, 1), (0, 3)]

    def other(offset):
        return lax.rem(row + offset[0], 4) * 4 + lax.rem(col + offset[1], 4)

    def square_copy(offset):
        return remote(own_square, squares.at[bond], square_send, square_sem, (core, site, other(offset)))

    def exchange_squares(value):
        own_square[...] = value
        squares[bond] = value
        for offset in far_first:
            square_copy(offset).start()

    def inverse_scale():
        pltpu.make_async_copy(squares.at[pl.ds(0, 15)], squares.at[pl.ds(0, 15)], square_sem).wait()
        total = jnp.sum(squares[...])
        mean = jnp.full((8, 128), total, F32) / 524288.0
        return 1.0 / jnp.sqrt(mean + 1e-06)

    def fold(value):
        squared = value * value
        acc = jnp.zeros((8, 128), F32)
        for r0 in range(0, value.shape[0], 8):
            for c0 in range(0, 512, 128):
                acc = acc + squared[r0:r0 + 8, c0:c0 + 128]
        return acc

    def write_out(inverse):
        pieces = []
        for r0 in (0, 8):
            for pair in range(2):
                for d_pair in range(4):
                    first = slab[2 * pair, r0:r0 + 8, d_pair * 128:d_pair * 128 + 128]
                    second = slab[2 * pair + 1, r0:r0 + 8, d_pair * 128:d_pair * 128 + 128]
                    lanes = slice(pair * 128, pair * 128 + 128)
                    pieces.append((2 * d_pair, r0, lanes, pair_even(first, second)))
                    pieces.append((2 * d_pair + 1, r0, lanes, pair_odd(first, second)))
        scale = inverse()
        for d, r0, lanes, value in pieces:
            out_ref[d, r0:r0 + 8, lanes] = value * scale

    def wait_squares_sent():
        pltpu.make_async_copy(squares.at[pl.ds(0, 15)], squares.at[pl.ds(0, 15)], square_send).wait()

    def wait_left_sent():
        for k in range(2):
            pltpu.make_async_copy(left_packed.at[k], left_packed.at[k], left_send.at[k]).wait()

    @pl.when(core == 0)
    def _():
        partner = (1, site, bond)
        for k in (0, 2):
            quarter = lax.rem(row + k, 4)
            lanes = pl.ds(pl.multiple_of(lax.rem(quarter, 2) * 128, 128), 128)
            size = 8 if k == 0 else 32
            for start in range(0, 32, size):
                rows = pl.ds(col * 64 + (quarter // 2) * 32 + start, size)
                remote(
                    p_ref.at[0, rows, :, lanes], first_left.at[quarter, pl.ds(start, size)], first_left_send,
                    lead_sem.at[start // 8] if k == 0 else first_left_sem, (1, next_site, bond),
                ).start()
        first_right = [
            remote(left_packed.at[0, pair], left_in.at[0, pair], left_send.at[0], left_sem.at[0, pair], partner)
            for pair in range(4)
        ]
        right_copy = remote(own_right(1), right_raw.at[1], right_send, right_sem.at[1], partner)
        mpo_copies = [remote(m_ref.at[k], mpo_raw.at[k], mpo_send.at[k], mpo_sem.at[k], partner) for k in range(2)]
        left_stage_copy(0).wait()
        for pair in range(4):
            pack_left(0, pair)
        pl.semaphore_wait(open_sem, 1)
        pl.semaphore_signal(ready_sem, inc=1, device_id=partner, device_id_type=MESH)
        for pair in range(4):
            first_right[pair].start()
        for k in range(2):
            mpo_copies[k].start()
        left_stage_copy(1).wait()
        for pair in range(4):
            pack_left(1, pair)
            left_send_copy(1, pair, 1).start()
        right_copy.start()
        pltpu.make_async_copy(slab, slab, slab_sem).wait()
        acc = jnp.zeros((8, 128), F32)
        for k in range(4):
            acc = acc + fold(slab[k])
        exchange_squares(acc)
        inverse = inverse_scale()
        scale_in[...] = inverse
        scale_copy = remote(scale_in, scale_in, scale_send, scale_sem, partner)
        scale_copy.start()
        write_out(lambda: inverse)
        scale_copy.wait_send()
        wait_squares_sent()
        wait_left_sent()
        right_copy.wait_send()
        for k in range(2):
            mpo_copies[k].wait_send()
        sent = first_left.at[pl.ds(0, 2)]
        pltpu.make_async_copy(sent, sent, first_left_send).wait()

    @pl.when(core == 1)
    def _():
        def prepare_left(lattice_row):
            for pair in range(4):
                pltpu.make_async_copy(
                    left_in.at[lattice_row, pair], left_in.at[lattice_row, pair], left_sem.at[lattice_row, pair]
                ).wait()
                high, low = halves(left_in[lattice_row, pair])
                left_high[:, pair * 128:pair * 128 + 128] = high
                left_low[:, pair * 128:pair * 128 + 128] = low

        def prepare_right(lattice_row):
            pltpu.make_async_copy(right_raw.at[lattice_row], right_raw.at[lattice_row], right_sem.at[lattice_row]).wait()
            turned = right_raw[lattice_row].reshape(512, 256).T
            starts = [target * 64 + piece * 8 for piece in range(8) for target in range(4)]
            turned = jnp.concatenate([turned[start:start + 8] for start in starts], axis=0)
            high, low = halves(turned)
            for c in range(4):
                lanes = slice(c * 128, c * 128 + 128)
                right_parts[c, :, 0:128] = high[:, lanes]
                right_parts[c, :, 128:256] = high[:, lanes]
                right_parts[c, :, 256:384] = low[:, lanes]
            pltpu.make_async_copy(mpo_raw.at[lattice_row], mpo_raw.at[lattice_row], mpo_sem.at[lattice_row]).wait()
            turned = jnp.concatenate([mpo_raw[lattice_row, :, d, :].T for d in range(8)], axis=0)
            high, low = halves(turned)
            mpo_parts[...] = jnp.concatenate([high, high, low], axis=1)

        def first_copy(offset):
            target = other(offset)
            return remote(
                first_packed.at[lax.rem(target, 4)], first_in.at[bond], first_send, first_sem, (1, site, target)
            )

        raw_copy = pltpu.make_async_copy(b_ref, first_raw, raw_sem)
        raw_copy.start()
        for k in range(2):
            pltpu.make_async_copy(own_right(k), right_raw.at[2 + k], right_sem.at[2 + k]).start()
            pltpu.make_async_copy(m_ref.at[k], mpo_raw.at[2 + k], mpo_sem.at[2 + k]).start()
        raw_copy.wait()
        for block in range(2):
            for u_pair in range(4):
                first = first_raw[2 * u_pair, :, block * 128:block * 128 + 128]
                second = first_raw[2 * u_pair + 1, :, block * 128:block * 128 + 128]
                lanes = slice(u_pair * 128, u_pair * 128 + 128)
                first_packed[2 * block, :, lanes] = pair_even(first, second)
                first_packed[2 * block + 1, :, lanes] = pair_odd(first, second)
        pltpu.make_async_copy(first_packed.at[col], first_in.at[bond], first_sem).start()
        pl.semaphore_wait(barrier, 16)
        pl.semaphore_signal(open_sem, inc=1, device_id=(0, site, bond), device_id_type=MESH)
        for offset in far_first:
            first_copy(offset).start()

        def mix_left(rows_high, rows_low):
            both = dot(jnp.concatenate([rows_high, rows_low], axis=0), left_high[...])
            return both[0:128] + both[128:256] + dot(rows_high, left_low[...])

        def mix_mpo(left_part, c):
            for pair in range(4):
                lanes = slice(pair * 128, pair * 128 + 128)
                first = left_part[0:64, lanes]
                second = left_part[64:128, lanes]
                even = pair_even(first, second)
                odd = pair_odd(first, second)
                for k in range(8):
                    block = slice(k * 128, k * 128 + 128)
                    mixed_in[c, pair * 16:pair * 16 + 8, block] = even[k * 8:k * 8 + 8]
                    mixed_in[c, pair * 16 + 8:pair * 16 + 16, block] = odd[k * 8:k * 8 + 8]
            high, low = halves(mixed_in[c])
            mixed = dot(mpo_parts[...], jnp.concatenate([high, low, high], axis=0))
            for pair in range(4):
                lanes = slice(pair * 128, pair * 128 + 128)
                for k in range(8):
                    block = slice(k * 128, k * 128 + 128)
                    first = mixed[pair * 16:pair * 16 + 8, block]
                    second = mixed[pair * 16 + 8:pair * 16 + 16, block]
                    mixed_out[c, k * 8:k * 8 + 8, lanes] = pair_even(first, second)
                    mixed_out[c, 64 + k * 8:64 + k * 8 + 8, lanes] = pair_odd(first, second)

        def close(lattice_row, c, start=0, size=256):
            high, low = halves(mixed_out[c])
            rows = slice(start, start + size)
            added = dot(right_parts[c, rows, :], jnp.concatenate([high, low, high], axis=0))
            if c == 0:
                partial[lattice_row, rows, :] = added
            else:
                partial[lattice_row, rows, :] += added

        def gather_copy(lattice_row, c, step):
            piece = gathered.at[lattice_row, c // 2, col, pl.ds(pl.multiple_of(lax.rem(c, 2) * 8, 8), 8)]
            return remote(
                piece, piece, gather_send.at[lattice_row], gather_sem.at[lattice_row, c // 2], (1, site, in_row(step))
            )

        def pass_on():
            for k in range(4):
                lead = first_left.at[row, pl.ds(k * 8, 8)]
                pltpu.make_async_copy(lead, lead, lead_sem.at[k]).wait()
                for step in (1, 3):
                    remote(lead, lead, lead_send, tail_sem, (1, site, in_col(step))).start()

        def close_first(k, block):
            right = jnp.concatenate(
                [first_left[block + half, :, l, :] for l in range(8) for half in (0, 2)], axis=0
            )
            right_high, right_low = halves(right)
            high, low = halves(mixed_out[...].reshape(512, 512))
            both = dot(jnp.concatenate([high, low], axis=0), right_high)
            first_out[k] = both[0:512] + both[512:1024] + dot(high, right_low)
            for d_pair in range(4):
                first = first_out[k, pl.ds(2 * d_pair, 64, stride=8), :]
                second = first_out[k, pl.ds(2 * d_pair + 1, 64, stride=8), :]
                lanes = slice(d_pair * 128, d_pair * 128 + 128)
                even = pair_even(first, second)
                odd = pair_odd(first, second)
                for piece in range(8):
                    start = pl.multiple_of(piece * 32 + block * 16, 16)
                    partial[0, pl.ds(start, 8), lanes] = even[piece * 8:piece * 8 + 8]
                    partial[0, pl.ds(pl.multiple_of(start + 8, 8), 8), lanes] = odd[piece * 8:piece * 8 + 8]

        def first_row():
            for pair in range(4):
                arrived = left_in.at[0, pair]
                pltpu.make_async_copy(arrived, arrived, left_sem.at[0, pair]).wait()
                turned = left_in[0, pair].T
                for k in range(2):
                    for block in range(2):
                        turned_rows[block, pl.ds(2 * pair + k, 64, stride=8), :] = (
                            turned[k * 64:k * 64 + 64, block * 128:block * 128 + 128]
                        )
            high, low = halves(jnp.concatenate([turned_rows[0], turned_rows[1]], axis=1))
            turned_high[...] = high
            turned_low[...] = low
            pltpu.make_async_copy(mpo_raw.at[0], mpo_raw.at[0], mpo_sem.at[0]).wait()
            turned = mpo_raw[0].reshape(8, 8, 8, 8)
            turned = jnp.concatenate([turned[:, u].reshape(64, 8) for u in range(8)], axis=1)
            high, low = halves(turned)
            mpo_parts[...] = jnp.concatenate([high, high, low], axis=1)
            for k in range(2):
                left_stage_copy(k).wait()
                for pair in range(4):
                    pack_left(k, pair)
            pass_on()
            pltpu.make_async_copy(first_in, first_in, first_sem).wait()
            high, low = halves(first_in[...].reshape(256, 512))
            left_high[...] = high
            left_low[...] = low
            parts = []
            for c in range(4):
                rows = slice(c * 128, c * 128 + 128)
                parts.append(mix_left(turned_high[rows, :], turned_low[rows, :]))
                if c > 0:
                    mix_mpo(parts[c - 1], c - 1)
            mix_mpo(parts[3], 3)
            near = lax.rem(row, 2)
            pltpu.make_async_copy(first_left.at[0], first_left.at[0], first_left_sem).wait()
            close_first(0, near)
            pltpu.make_async_copy(first_left.at[pl.ds(0, 2)], first_left.at[pl.ds(0, 2)], tail_sem).wait()
            close_first(1, 1 - near)

        def place_rows(lattice_row, c):
            source = lattice_row - 1
            three = gathered.at[source, c, pl.ds(0, 3)]
            pltpu.make_async_copy(three, three, gather_sem.at[source, c]).wait()
            for r0 in (0, 8):
                for pair in range(2):
                    for u_pair in range(4):
                        block = slice(u_pair * 128, u_pair * 128 + 128)
                        first = gathered[source, c, 2 * pair, r0:r0 + 8, block]
                        second = gathered[source, c, 2 * pair + 1, r0:r0 + 8, block]
                        start = r0 * 8 + 2 * u_pair
                        lhs_rows[pair, pl.ds(start, 8, stride=8), :] = pair_even(first, second)
                        lhs_rows[pair, pl.ds(start + 1, 8, stride=8), :] = pair_odd(first, second)
            return halves(jnp.concatenate([lhs_rows[0], lhs_rows[1]], axis=1))

        def later_row(lattice_row):
            for c in range(4):
                high, low = place_rows(lattice_row, c)
                left_part = mix_left(high, low)
                if c > 0:
                    close(lattice_row, c - 1)
                mix_mpo(left_part, c)
            close(lattice_row, 3, 0, 64)
            send_partial(lattice_row, 0, 2)
            close(lattice_row, 3, 64, 192)
            send_partial(lattice_row, 2, 8)

        def partial_copy(lattice_row, c, step):
            is_first = lattice_row == 0
            target = lax.rem(jnp.where(is_first, col, row) + step, 4)
            rows = pl.ds(pl.multiple_of(c * 32 + target * 8, 8), 8)
            device = jnp.where(is_first, in_row(step), in_col(step))
            return remote(
                partial.at[lattice_row, rows], partial_in.at[lattice_row, c, step - 1],
                partial_send.at[lattice_row], partial_sem.at[lattice_row, c], (1, site, device),
            )

        def send_partial(lattice_row, begin, end):
            @pl.loop(begin, end)
            def _(c):
                for step in (2, 1, 3):
                    partial_copy(lattice_row, c, step).start()

        def reduced(lattice_row, c):
            every = partial_in.at[lattice_row, c]
            pltpu.make_async_copy(every, every, partial_sem.at[lattice_row, c]).wait()
            own = jnp.where(lattice_row == 0, col, row)
            rows = pl.ds(pl.multiple_of(c * 32 + own * 8, 8), 8)
            total = partial[lattice_row, rows, :]
            for k in range(3):
                total = total + partial_in[lattice_row, c, k]
            return total

        def slab_out():
            return remote(gathered.at[1, col], slab, slab_send, slab_sem, (0, site, bond))

        def final_copy(c):
            return remote(gathered.at[3, c, col], slab.at[col], slab_send, slab_sem, (1, site, row * 4 + c))

        @pl.loop(0, 4)
        def _(lattice_row):
            @pl.when(lattice_row == 0)
            def _():
                first_row()
                send_partial(0, 0, 8)

            @pl.when(lattice_row > 0)
            def _():
                later_row(lattice_row)

            @pl.when(lattice_row == 0)
            def _():
                pl.semaphore_wait(ready_sem, 1)

            @pl.when(lattice_row < 2)
            def _():
                for pair in range(4):
                    left_send_copy(lattice_row, pair, lattice_row + 2).start()

            @pl.when(lattice_row == 2)
            def _():
                slab_out().start()

            @pl.when(lattice_row < 3)
            def _():
                prepare_right(lattice_row + 1)

                @pl.loop(0, 8)
                def _(c):
                    rows = pl.ds(pl.multiple_of(lax.rem(c, 2) * 8, 8), 8)
                    gathered[lattice_row, c // 2, col, rows, :] = reduced(lattice_row, c)
                    for step in (2, 1, 3):
                        gather_copy(lattice_row, c, step).start()

                prepare_left(lattice_row + 1)

        slab_out().wait_send()
        pltpu.make_async_copy(first_left.at[pl.ds(0, 2)], first_left.at[pl.ds(0, 2)], lead_send).wait()
        pltpu.make_async_copy(scale_in, scale_in, scale_sem).wait()
        inverse = scale_in[0:1, 0:1]
        acc = jnp.zeros((8, 128), F32)
        for c in range(4):
            total = jnp.concatenate([reduced(3, 2 * c), reduced(3, 2 * c + 1)], axis=0) * inverse
            acc = acc + fold(total)

            @pl.when(col == c)
            def _():
                slab[c] = total

            @pl.when(col != c)
            def _():
                gathered[3, c, col] = total
                if c < 3:
                    final_copy(c).start()

        exchange_squares(acc)

        @pl.when(col != 3)
        def _():
            final_copy(3).start()

        three = slab.at[pl.ds(0, 3)]
        pltpu.make_async_copy(three, three, slab_sem).wait()
        write_out(inverse_scale)

        pltpu.make_async_copy(three, three, slab_send).wait()
        wait_squares_sent()
        wait_left_sent()
        pltpu.make_async_copy(first_in.at[pl.ds(0, 15)], first_in.at[pl.ds(0, 15)], first_send).wait()
        for k in range(4):
            sent = partial.at[k, pl.ds(0, 192)]
            pltpu.make_async_copy(sent, sent, partial_send.at[k]).wait()
        for k in range(3):
            sent = gathered.at[k, pl.ds(0, 3)]
            pltpu.make_async_copy(sent, sent, gather_send.at[k]).wait()


def body(boundary_in, mpo, proj):
    b = jnp.transpose(boundary_in[0, 0], (1, 2, 0))
    m = mpo.reshape(2, 64, 8, 8)
    p = proj.reshape(2, 256, 8, 256)
    b, m, p = (pltpu.with_memory_space_constraint(v, pltpu.HBM) for v in (b, m, p))
    dma = pltpu.SemaphoreType.DMA
    out = pl.pallas_call(
        kernel,
        out_shape=jax.ShapeDtypeStruct((8, 16, 256), F32),
        in_specs=[pl.BlockSpec(memory_space=pltpu.HBM)] * 3,
        out_specs=pl.BlockSpec(memory_space=pltpu.VMEM),
        scratch_shapes=[
            pltpu.VMEM((8, 16, 256), F32),
            pltpu.VMEM((4, 16, 512), F32),
            pltpu.VMEM((16, 16, 512), F32),
            pltpu.VMEM((4, 32, 8, 128), F32),
            pltpu.VMEM((2, 512, 128), F32),
            pltpu.VMEM((2, 512, 128), F32),
            pltpu.VMEM((4, 4, 4, 16, 512), F32),
            pltpu.VMEM((4, 8, 3, 8, 512), F32),
            pltpu.VMEM((4, 256, 512), F32),
            pltpu.VMEM((4, 16, 512), F32),
            pltpu.VMEM((16, 8, 128), F32),
            pltpu.VMEM((8, 128), F32),
            pltpu.VMEM((8, 128), F32),
            pltpu.VMEM((2, 256, 8, 128), F32),
            pltpu.VMEM((2, 4, 256, 128), F32),
            pltpu.VMEM((4, 4, 256, 128), F32),
            pltpu.VMEM((4, 64, 8, 256), F32),
            pltpu.VMEM((4, 64, 8, 8), F32),
            pltpu.VMEM((256, 512), BF16),
            pltpu.VMEM((256, 512), BF16),
            pltpu.VMEM((512, 256), BF16),
            pltpu.VMEM((512, 256), BF16),
            pltpu.VMEM((4, 256, 384), BF16),
            pltpu.VMEM((64, 192), BF16),
            pltpu.VMEM((2, 128, 128), F32),
            pltpu.VMEM((4, 64, 1024), F32),
            pltpu.VMEM((4, 128, 512), F32),
            dma, dma, dma, dma, dma((4,)), dma, dma, pltpu.SemaphoreType.REGULAR,
            dma((3, 4)), dma((4, 8)), dma, dma, dma,
            dma((4, 4)), dma((4,)), dma((4,)), dma((2,)),
            pltpu.SemaphoreType.REGULAR,
            dma, dma((3,)), dma((4,)), dma, dma, dma,
            dma((2,)), dma, dma((2,)),
        ],
        compiler_params=pltpu.CompilerParams(
            collective_id=0, has_side_effects=True, vmem_limit_bytes=40 * 1024 * 1024
        ),
        name="absorb",
    )(b, p, m)
    return jnp.transpose(out, (2, 0, 1))[None, None, None]


def solution(mesh):
    return jax.shard_map(
        body,
        mesh=mesh,
        in_specs=(
            P(None, "sites", None, None, "bond"),
            P("rows", "sites", None, None, None, None),
            P("rows", "sites", None, None, None),
        ),
        out_specs=P("rows", None, "sites", None, None, "bond"),
        check_vma=False,
    )
```

```python
import functools

import jax
import jax.numpy as jnp
from jax import lax
from jax.experimental import pallas as pl
from jax.experimental.pallas import tpu as pltpu
from jax.sharding import PartitionSpec as P

MESH = pl.DeviceIdType.MESH
F32 = jnp.float32
BF16 = jnp.bfloat16


def halves(value):
    high = value.astype(BF16)
    return high, (value - high.astype(F32)).astype(BF16)


def dot(lhs, rhs):
    return jnp.dot(lhs, rhs, preferred_element_type=F32)


def low_lanes(rows):
    return lax.broadcasted_iota(jnp.int32, (rows, 128), 1) < 64


def pair_even(first, second):
    return jnp.where(low_lanes(first.shape[0]), first, pltpu.roll(second, 64, 1))


def pair_odd(first, second):
    return jnp.where(low_lanes(first.shape[0]), pltpu.roll(first, 64, 1), second)


def kernel(
    b_ref, p_ref, m_ref, out_ref,
    first_raw, first_packed, first_in, first_left, first_out, turned_rows, gathered, partial_in, partial, slab, squares, own_square, scale_in,
    left_stage, left_packed, left_in, right_raw, mpo_raw,
    left_high, left_low, turned_high, turned_low, right_parts, mpo_parts, lhs_rows, mixed_in, mixed_out,
    raw_sem, first_sem, first_left_sem, first_left_send, lead_sem, lead_send, tail_sem, open_sem,
    gather_sem, partial_sem, slab_sem, square_sem, scale_sem,
    left_sem, right_sem, mpo_sem, stage_sem,
    ready_sem, first_send, gather_send, partial_send, slab_send, square_send, scale_send,
    left_send, right_send, mpo_send,
):
    core = lax.axis_index("rows")
    site = lax.axis_index("sites")
    bond = lax.axis_index("bond")
    col = lax.rem(bond, 4)
    row = bond // 4
    next_site = lax.rem(site + 1, 8)
    prev_site = lax.rem(site + 7, 8)

    def in_row(step):
        return row * 4 + lax.rem(col + step, 4)

    def in_col(step):
        return lax.rem(row + step, 4) * 4 + col

    def remote(src, dst, send, recv, device):
        return pltpu.make_async_remote_copy(
            src_ref=src, dst_ref=dst, send_sem=send, recv_sem=recv, device_id=device, device_id_type=MESH
        )

    def left_stage_copy(k):
        part = jnp.where((core == 0) & (k == 0), row, col)
        block = pl.ds(pl.multiple_of((part // 2) * 128, 128), 128)
        return pltpu.make_async_copy(p_ref.at[k, :, :, block], left_stage.at[k], stage_sem.at[k])

    def own_right(k):
        return p_ref.at[k, pl.ds(row * 64, 64)]

    barrier = pltpu.get_barrier_semaphore()
    for k in range(2):
        left_stage_copy(k).start()

    def greet(device):
        pl.semaphore_signal(barrier, inc=1, device_id=device, device_id_type=MESH)

    @pl.when(core == 0)
    def _():
        greet((1, site, bond))
        pl.semaphore_wait(barrier, 1)

    @pl.when(core == 1)
    def _():
        greet((0, prev_site, bond))
        for step in range(1, 16):
            greet((1, site, lax.rem(bond + step, 16)))

    def left_send_copy(k, pair, lattice_row):
        return remote(
            left_packed.at[k, pair], left_in.at[lattice_row, pair], left_send.at[k], left_sem.at[lattice_row, pair],
            (1, next_site, bond),
        )

    def pack_left(k, pair):
        first = left_stage[k, :, 2 * pair, :]
        second = left_stage[k, :, 2 * pair + 1, :]
        half = lax.rem(jnp.where((core == 0) & (k == 0), row, col), 2)

        @pl.when(half == 0)
        def _():
            left_packed[k, pair] = pair_even(first, second)

        @pl.when(half == 1)
        def _():
            left_packed[k, pair] = pair_odd(first, second)

    far_first = [(2, 2), (2, 1), (2, 3), (1, 2), (3, 2), (1, 1), (1, 3), (3, 1), (3, 3), (2, 0), (0, 2), (1, 0), (3, 0), (0, 1), (0, 3)]

    def other(offset):
        return lax.rem(row + offset[0], 4) * 4 + lax.rem(col + offset[1], 4)

    def square_copy(offset):
        return remote(own_square, squares.at[bond], square_send, square_sem, (core, site, other(offset)))

    def exchange_squares(value):
        own_square[...] = value
        squares[bond] = value
        for offset in far_first:
            square_copy(offset).start()

    def inverse_scale():
        pltpu.make_async_copy(squares.at[pl.ds(0, 15)], squares.at[pl.ds(0, 15)], square_sem).wait()
        total = jnp.sum(squares[...])
        mean = jnp.full((8, 128), total, F32) / 524288.0
        return 1.0 / jnp.sqrt(mean + 1e-06)

    def fold(value):
        squared = value * value
        acc = jnp.zeros((8, 128), F32)
        for r0 in range(0, value.shape[0], 8):
            for c0 in range(0, 512, 128):
                acc = acc + squared[r0:r0 + 8, c0:c0 + 128]
        return acc

    def write_out(inverse):
        pieces = []
        for r0 in (0, 8):
            for pair in range(2):
                for d_pair in range(4):
                    first = slab[2 * pair, r0:r0 + 8, d_pair * 128:d_pair * 128 + 128]
                    second = slab[2 * pair + 1, r0:r0 + 8, d_pair * 128:d_pair * 128 + 128]
                    lanes = slice(pair * 128, pair * 128 + 128)
                    pieces.append((2 * d_pair, r0, lanes, pair_even(first, second)))
                    pieces.append((2 * d_pair + 1, r0, lanes, pair_odd(first, second)))
        scale = inverse()
        for d, r0, lanes, value in pieces:
            out_ref[d, r0:r0 + 8, lanes] = value * scale

    def wait_squares_sent():
        pltpu.make_async_copy(squares.at[pl.ds(0, 15)], squares.at[pl.ds(0, 15)], square_send).wait()

    def wait_left_sent():
        for k in range(2):
            pltpu.make_async_copy(left_packed.at[k], left_packed.at[k], left_send.at[k]).wait()

    @pl.when(core == 0)
    def _():
        partner = (1, site, bond)
        for k in (0, 2):
            quarter = lax.rem(row + k, 4)
            lanes = pl.ds(pl.multiple_of(lax.rem(quarter, 2) * 128, 128), 128)
            size = 8 if k == 0 else 32
            for start in range(0, 32, size):
                rows = pl.ds(col * 64 + (quarter // 2) * 32 + start, size)
                remote(
                    p_ref.at[0, rows, :, lanes], first_left.at[quarter, pl.ds(start, size)], first_left_send,
                    lead_sem.at[start // 8] if k == 0 else first_left_sem, (1, next_site, bond),
                ).start()
        first_right = [
            remote(left_packed.at[0, pair], left_in.at[0, pair], left_send.at[0], left_sem.at[0, pair], partner)
            for pair in range(4)
        ]
        right_copy = remote(own_right(1), right_raw.at[1], right_send, right_sem.at[1], partner)
        mpo_copies = [remote(m_ref.at[k], mpo_raw.at[k], mpo_send.at[k], mpo_sem.at[k], partner) for k in range(2)]
        left_stage_copy(0).wait()
        for pair in range(4):
            pack_left(0, pair)
        pl.semaphore_wait(open_sem, 1)
        pl.semaphore_signal(ready_sem, inc=1, device_id=partner, device_id_type=MESH)
        for pair in range(4):
            first_right[pair].start()
        for k in range(2):
            mpo_copies[k].start()
        left_stage_copy(1).wait()
        for pair in range(4):
            pack_left(1, pair)
            left_send_copy(1, pair, 1).start()
        right_copy.start()
        pltpu.make_async_copy(slab, slab, slab_sem).wait()
        acc = jnp.zeros((8, 128), F32)
        for k in range(4):
            acc = acc + fold(slab[k])
        exchange_squares(acc)
        inverse = inverse_scale()
        scale_in[...] = inverse
        scale_copy = remote(scale_in, scale_in, scale_send, scale_sem, partner)
        scale_copy.start()
        write_out(lambda: inverse)
        scale_copy.wait_send()
        wait_squares_sent()
        wait_left_sent()
        right_copy.wait_send()
        for k in range(2):
            mpo_copies[k].wait_send()
        sent = first_left.at[pl.ds(0, 2)]
        pltpu.make_async_copy(sent, sent, first_left_send).wait()

    @pl.when(core == 1)
    def _():
        def prepare_left(lattice_row):
            for pair in range(4):
                pltpu.make_async_copy(
                    left_in.at[lattice_row, pair], left_in.at[lattice_row, pair], left_sem.at[lattice_row, pair]
                ).wait()
                high, low = halves(left_in[lattice_row, pair])
                left_high[:, pair * 128:pair * 128 + 128] = high
                left_low[:, pair * 128:pair * 128 + 128] = low

        def prepare_right(lattice_row):
            pltpu.make_async_copy(right_raw.at[lattice_row], right_raw.at[lattice_row], right_sem.at[lattice_row]).wait()
            turned = right_raw[lattice_row].reshape(512, 256).T
            starts = [target * 64 + piece * 8 for piece in range(8) for target in range(4)]
            turned = jnp.concatenate([turned[start:start + 8] for start in starts], axis=0)
            high, low = halves(turned)
            for c in range(4):
                lanes = slice(c * 128, c * 128 + 128)
                right_parts[c, :, 0:128] = high[:, lanes]
                right_parts[c, :, 128:256] = high[:, lanes]
                right_parts[c, :, 256:384] = low[:, lanes]
            pltpu.make_async_copy(mpo_raw.at[lattice_row], mpo_raw.at[lattice_row], mpo_sem.at[lattice_row]).wait()
            turned = jnp.concatenate([mpo_raw[lattice_row, :, d, :].T for d in range(8)], axis=0)
            high, low = halves(turned)
            mpo_parts[...] = jnp.concatenate([high, high, low], axis=1)

        def first_copy(offset):
            target = other(offset)
            return remote(
                first_packed.at[lax.rem(target, 4)], first_in.at[bond], first_send, first_sem, (1, site, target)
            )

        raw_copy = pltpu.make_async_copy(b_ref, first_raw, raw_sem)
        raw_copy.start()
        for k in range(2):
            pltpu.make_async_copy(own_right(k), right_raw.at[2 + k], right_sem.at[2 + k]).start()
            pltpu.make_async_copy(m_ref.at[k], mpo_raw.at[2 + k], mpo_sem.at[2 + k]).start()
        raw_copy.wait()
        for block in range(2):
            for u_pair in range(4):
                first = first_raw[2 * u_pair, :, block * 128:block * 128 + 128]
                second = first_raw[2 * u_pair + 1, :, block * 128:block * 128 + 128]
                lanes = slice(u_pair * 128, u_pair * 128 + 128)
                first_packed[2 * block, :, lanes] = pair_even(first, second)
                first_packed[2 * block + 1, :, lanes] = pair_odd(first, second)
        pltpu.make_async_copy(first_packed.at[col], first_in.at[bond], first_sem).start()
        pl.semaphore_wait(barrier, 16)
        pl.semaphore_signal(open_sem, inc=1, device_id=(0, site, bond), device_id_type=MESH)
        for offset in far_first:
            first_copy(offset).start()

        def mix_left(rows_high, rows_low):
            both = dot(jnp.concatenate([rows_high, rows_low], axis=0), left_high[...])
            return both[0:128] + both[128:256] + dot(rows_high, left_low[...])

        def mix_mpo(left_part, c):
            for pair in range(4):
                lanes = slice(pair * 128, pair * 128 + 128)
                first = left_part[0:64, lanes]
                second = left_part[64:128, lanes]
                even = pair_even(first, second)
                odd = pair_odd(first, second)
                for k in range(8):
                    block = slice(k * 128, k * 128 + 128)
                    mixed_in[c, pair * 16:pair * 16 + 8, block] = even[k * 8:k * 8 + 8]
                    mixed_in[c, pair * 16 + 8:pair * 16 + 16, block] = odd[k * 8:k * 8 + 8]
            high, low = halves(mixed_in[c])
            mixed = dot(mpo_parts[...], jnp.concatenate([high, low, high], axis=0))
            for pair in range(4):
                lanes = slice(pair * 128, pair * 128 + 128)
                for k in range(8):
                    block = slice(k * 128, k * 128 + 128)
                    first = mixed[pair * 16:pair * 16 + 8, block]
                    second = mixed[pair * 16 + 8:pair * 16 + 16, block]
                    mixed_out[c, k * 8:k * 8 + 8, lanes] = pair_even(first, second)
                    mixed_out[c, 64 + k * 8:64 + k * 8 + 8, lanes] = pair_odd(first, second)

        def close(lattice_row, c, start=0, size=256):
            high, low = halves(mixed_out[c])
            rows = slice(start, start + size)
            added = dot(right_parts[c, rows, :], jnp.concatenate([high, low, high], axis=0))
            if c == 0:
                partial[lattice_row, rows, :] = added
            else:
                partial[lattice_row, rows, :] += added

        def gather_copy(lattice_row, c, step):
            piece = gathered.at[lattice_row, c // 2, col, pl.ds(pl.multiple_of(lax.rem(c, 2) * 8, 8), 8)]
            return remote(
                piece, piece, gather_send.at[lattice_row], gather_sem.at[lattice_row, c], (1, site, in_row(step))
            )

        def pass_on():
            for k in range(4):
                lead = first_left.at[row, pl.ds(k * 8, 8)]
                pltpu.make_async_copy(lead, lead, lead_sem.at[k]).wait()
                for step in (1, 3):
                    remote(lead, lead, lead_send, tail_sem, (1, site, in_col(step))).start()

        def close_first(k, block):
            right = jnp.concatenate(
                [first_left[block + half, :, l, :] for l in range(8) for half in (0, 2)], axis=0
            )
            right_high, right_low = halves(right)
            high, low = halves(mixed_out[...].reshape(512, 512))
            both = dot(jnp.concatenate([high, low], axis=0), right_high)
            first_out[k] = both[0:512] + both[512:1024] + dot(high, right_low)
            for d_pair in range(4):
                first = first_out[k, pl.ds(2 * d_pair, 64, stride=8), :]
                second = first_out[k, pl.ds(2 * d_pair + 1, 64, stride=8), :]
                lanes = slice(d_pair * 128, d_pair * 128 + 128)
                even = pair_even(first, second)
                odd = pair_odd(first, second)
                for piece in range(8):
                    start = pl.multiple_of(piece * 32 + block * 16, 16)
                    partial[0, pl.ds(start, 8), lanes] = even[piece * 8:piece * 8 + 8]
                    partial[0, pl.ds(pl.multiple_of(start + 8, 8), 8), lanes] = odd[piece * 8:piece * 8 + 8]

        def first_row():
            for pair in range(4):
                arrived = left_in.at[0, pair]
                pltpu.make_async_copy(arrived, arrived, left_sem.at[0, pair]).wait()
                turned = left_in[0, pair].T
                for k in range(2):
                    for block in range(2):
                        turned_rows[block, pl.ds(2 * pair + k, 64, stride=8), :] = (
                            turned[k * 64:k * 64 + 64, block * 128:block * 128 + 128]
                        )
            high, low = halves(jnp.concatenate([turned_rows[0], turned_rows[1]], axis=1))
            turned_high[...] = high
            turned_low[...] = low
            pltpu.make_async_copy(mpo_raw.at[0], mpo_raw.at[0], mpo_sem.at[0]).wait()
            turned = mpo_raw[0].reshape(8, 8, 8, 8)
            turned = jnp.concatenate([turned[:, u].reshape(64, 8) for u in range(8)], axis=1)
            high, low = halves(turned)
            mpo_parts[...] = jnp.concatenate([high, high, low], axis=1)
            for k in range(2):
                left_stage_copy(k).wait()
                for pair in range(4):
                    pack_left(k, pair)
            pass_on()
            pltpu.make_async_copy(first_in, first_in, first_sem).wait()
            high, low = halves(first_in[...].reshape(256, 512))
            left_high[...] = high
            left_low[...] = low
            parts = []
            for c in range(4):
                rows = slice(c * 128, c * 128 + 128)
                parts.append(mix_left(turned_high[rows, :], turned_low[rows, :]))
                if c > 0:
                    mix_mpo(parts[c - 1], c - 1)
            mix_mpo(parts[3], 3)
            near = lax.rem(row, 2)
            pltpu.make_async_copy(first_left.at[0], first_left.at[0], first_left_sem).wait()
            close_first(0, near)
            pltpu.make_async_copy(first_left.at[pl.ds(0, 2)], first_left.at[pl.ds(0, 2)], tail_sem).wait()
            close_first(1, 1 - near)

        def place_rows(lattice_row, c):
            source = lattice_row - 1
            for r0 in (0, 8):
                three = gathered.at[source, c, pl.ds(0, 3), pl.ds(r0, 8)]
                pltpu.make_async_copy(three, three, gather_sem.at[source, 2 * c + r0 // 8]).wait()
                for pair in range(2):
                    for u_pair in range(4):
                        block = slice(u_pair * 128, u_pair * 128 + 128)
                        first = gathered[source, c, 2 * pair, r0:r0 + 8, block]
                        second = gathered[source, c, 2 * pair + 1, r0:r0 + 8, block]
                        start = r0 * 8 + 2 * u_pair
                        lhs_rows[pair, pl.ds(start, 8, stride=8), :] = pair_even(first, second)
                        lhs_rows[pair, pl.ds(start + 1, 8, stride=8), :] = pair_odd(first, second)
            return halves(jnp.concatenate([lhs_rows[0], lhs_rows[1]], axis=1))

        def later_row(lattice_row):
            for c in range(4):
                high, low = place_rows(lattice_row, c)
                left_part = mix_left(high, low)
                if c > 0:
                    close(lattice_row, c - 1)
                mix_mpo(left_part, c)
            close(lattice_row, 3, 0, 64)
            send_partial(lattice_row, 0, 2)
            close(lattice_row, 3, 64, 192)
            send_partial(lattice_row, 2, 8)

        def partial_copy(lattice_row, c, step):
            is_first = lattice_row == 0
            target = lax.rem(jnp.where(is_first, col, row) + step, 4)
            rows = pl.ds(pl.multiple_of(c * 32 + target * 8, 8), 8)
            device = jnp.where(is_first, in_row(step), in_col(step))
            return remote(
                partial.at[lattice_row, rows], partial_in.at[lattice_row, c, step - 1],
                partial_send.at[lattice_row], partial_sem.at[lattice_row, c], (1, site, device),
            )

        def send_partial(lattice_row, begin, end):
            @pl.loop(begin, end)
            def _(c):
                for step in (2, 1, 3):
                    partial_copy(lattice_row, c, step).start()

        def reduced(lattice_row, c):
            every = partial_in.at[lattice_row, c]
            pltpu.make_async_copy(every, every, partial_sem.at[lattice_row, c]).wait()
            own = jnp.where(lattice_row == 0, col, row)
            rows = pl.ds(pl.multiple_of(c * 32 + own * 8, 8), 8)
            total = partial[lattice_row, rows, :]
            for k in range(3):
                total = total + partial_in[lattice_row, c, k]
            return total

        def slab_out():
            return remote(gathered.at[1, col], slab, slab_send, slab_sem, (0, site, bond))

        def final_copy(c):
            return remote(gathered.at[3, c, col], slab.at[col], slab_send, slab_sem, (1, site, row * 4 + c))

        @pl.loop(0, 4)
        def _(lattice_row):
            @pl.when(lattice_row == 0)
            def _():
                first_row()
                send_partial(0, 0, 8)

            @pl.when(lattice_row > 0)
            def _():
                later_row(lattice_row)

            @pl.when(lattice_row == 0)
            def _():
                pl.semaphore_wait(ready_sem, 1)

            @pl.when(lattice_row < 2)
            def _():
                for pair in range(4):
                    left_send_copy(lattice_row, pair, lattice_row + 2).start()

            @pl.when(lattice_row == 2)
            def _():
                slab_out().start()

            @pl.when(lattice_row < 3)
            def _():
                prepare_right(lattice_row + 1)

                @pl.loop(0, 8)
                def _(c):
                    rows = pl.ds(pl.multiple_of(lax.rem(c, 2) * 8, 8), 8)
                    gathered[lattice_row, c // 2, col, rows, :] = reduced(lattice_row, c)
                    for step in (2, 1, 3):
                        gather_copy(lattice_row, c, step).start()

                prepare_left(lattice_row + 1)

        slab_out().wait_send()
        pltpu.make_async_copy(first_left.at[pl.ds(0, 2)], first_left.at[pl.ds(0, 2)], lead_send).wait()
        pltpu.make_async_copy(scale_in, scale_in, scale_sem).wait()
        inverse = scale_in[0:1, 0:1]
        acc = jnp.zeros((8, 128), F32)
        for c in range(4):
            total = jnp.concatenate([reduced(3, 2 * c), reduced(3, 2 * c + 1)], axis=0) * inverse
            acc = acc + fold(total)

            @pl.when(col == c)
            def _():
                slab[c] = total

            @pl.when(col != c)
            def _():
                gathered[3, c, col] = total
                if c < 3:
                    final_copy(c).start()

        exchange_squares(acc)

        @pl.when(col != 3)
        def _():
            final_copy(3).start()

        three = slab.at[pl.ds(0, 3)]
        pltpu.make_async_copy(three, three, slab_sem).wait()
        write_out(inverse_scale)

        pltpu.make_async_copy(three, three, slab_send).wait()
        wait_squares_sent()
        wait_left_sent()
        pltpu.make_async_copy(first_in.at[pl.ds(0, 15)], first_in.at[pl.ds(0, 15)], first_send).wait()
        for k in range(4):
            sent = partial.at[k, pl.ds(0, 192)]
            pltpu.make_async_copy(sent, sent, partial_send.at[k]).wait()
        for k in range(3):
            sent = gathered.at[k, pl.ds(0, 3)]
            pltpu.make_async_copy(sent, sent, gather_send.at[k]).wait()


def body(boundary_in, mpo, proj):
    b = jnp.transpose(boundary_in[0, 0], (1, 2, 0))
    m = mpo.reshape(2, 64, 8, 8)
    p = proj.reshape(2, 256, 8, 256)
    b, m, p = (pltpu.with_memory_space_constraint(v, pltpu.HBM) for v in (b, m, p))
    dma = pltpu.SemaphoreType.DMA
    out = pl.pallas_call(
        kernel,
        out_shape=jax.ShapeDtypeStruct((8, 16, 256), F32),
        in_specs=[pl.BlockSpec(memory_space=pltpu.HBM)] * 3,
        out_specs=pl.BlockSpec(memory_space=pltpu.VMEM),
        scratch_shapes=[
            pltpu.VMEM((8, 16, 256), F32),
            pltpu.VMEM((4, 16, 512), F32),
            pltpu.VMEM((16, 16, 512), F32),
            pltpu.VMEM((4, 32, 8, 128), F32),
            pltpu.VMEM((2, 512, 128), F32),
            pltpu.VMEM((2, 512, 128), F32),
            pltpu.VMEM((4, 4, 4, 16, 512), F32),
            pltpu.VMEM((4, 8, 3, 8, 512), F32),
            pltpu.VMEM((4, 256, 512), F32),
            pltpu.VMEM((4, 16, 512), F32),
            pltpu.VMEM((16, 8, 128), F32),
            pltpu.VMEM((8, 128), F32),
            pltpu.VMEM((8, 128), F32),
            pltpu.VMEM((2, 256, 8, 128), F32),
            pltpu.VMEM((2, 4, 256, 128), F32),
            pltpu.VMEM((4, 4, 256, 128), F32),
            pltpu.VMEM((4, 64, 8, 256), F32),
            pltpu.VMEM((4, 64, 8, 8), F32),
            pltpu.VMEM((256, 512), BF16),
            pltpu.VMEM((256, 512), BF16),
            pltpu.VMEM((512, 256), BF16),
            pltpu.VMEM((512, 256), BF16),
            pltpu.VMEM((4, 256, 384), BF16),
            pltpu.VMEM((64, 192), BF16),
            pltpu.VMEM((2, 128, 128), F32),
            pltpu.VMEM((4, 64, 1024), F32),
            pltpu.VMEM((4, 128, 512), F32),
            dma, dma, dma, dma, dma((4,)), dma, dma, pltpu.SemaphoreType.REGULAR,
            dma((3, 8)), dma((4, 8)), dma, dma, dma,
            dma((4, 4)), dma((4,)), dma((4,)), dma((2,)),
            pltpu.SemaphoreType.REGULAR,
            dma, dma((3,)), dma((4,)), dma, dma, dma,
            dma((2,)), dma, dma((2,)),
        ],
        compiler_params=pltpu.CompilerParams(
            collective_id=0, has_side_effects=True, vmem_limit_bytes=40 * 1024 * 1024
        ),
        name="absorb",
    )(b, p, m)
    return jnp.transpose(out, (2, 0, 1))[None, None, None]


def solution(mesh):
    return jax.shard_map(
        body,
        mesh=mesh,
        in_specs=(
            P(None, "sites", None, None, "bond"),
            P("rows", "sites", None, None, None, None),
            P("rows", "sites", None, None, None),
        ),
        out_specs=P("rows", None, "sites", None, None, "bond"),
        check_vma=False,
    )
```
